128 devices in a mesh: dp: 4 (over y), seq: 32 (over z, x, core).
Axes of the slice: x: 4, y: 4, z: 4, core: 2. Of those that a mesh axis runs over, the one named last changes fastest.
Arguments:
- queries: bfloat16 [4, 32768, 2048], P('dp', 'seq'), may hold values from -420 to 420
- keys: bfloat16 [4, 32768, 2048], P('dp', 'seq'), may hold values from -24 to 24
- values: bfloat16 [4, 32768, 2048], P('dp', 'seq'), may hold values from -12 to 12
- codes: int32 [4, 16, 32768], P('dp', None, 'seq'), may hold values from 0 to 511
- starts: int32 [4, 64], P('dp', 'seq'), may hold values from 0 to 1
- old_centroids: float32 [16, 512, 128], replicated, may hold values from -6 to 6
- old_counts: float32 [16, 512], replicated, may hold values from 4 to 64
Outputs:
- mixed: bfloat16 [4, 32768, 2048], P('dp', 'seq')
- codebook: float32 [16, 512, 128], P(None, 'dp')
The draws below stay inside these ranges and needn't reach their ends.
All inputs are finite; a program needn't handle non-finite values.
Results may differ from the reference program's by a relative error of at most 0.0034.
Values sent between devices are 32-bit elements; how exact they have to be, the bound alone decides.
A program may use at most 384 MiB of HBM per device.

```python
import math
import jax
import jax.numpy as jnp
from jax import lax

HEADS = 16
HEAD_DIM = 128
CODES = 512
BLOCK = 512
WIDTH = 2048
LENGTH = 32768
BATCH = 4
SEQ_BLOCKS = 64


def draw_queries(key, part):
    shape_all = (BATCH, LENGTH, WIDTH)
    drawn = 2.0 * jax.random.truncated_normal(key, -8.0, 8.0, shape_all, jnp.float32)
    return drawn.astype(jnp.bfloat16)


def draw_values(key, part):
    level_key = jax.random.fold_in(key, 11)
    sign_key = jax.random.fold_in(key, 12)
    noise_key = jax.random.fold_in(key, 13)
    level_shape = (BATCH, 4, 1, WIDTH)
    noise_shape = (BATCH, 4, LENGTH // 4, WIDTH)
    signs = jnp.where(jax.random.bernoulli(sign_key, 0.5, level_shape), 1.0, -1.0)
    magnitude = jax.random.uniform(level_key, level_shape, jnp.float32, 1.0, 2.5)
    noise = 1.5 * jax.random.truncated_normal(noise_key, -6.0, 6.0, noise_shape, jnp.float32)
    drawn = (signs * magnitude + noise).reshape(BATCH, LENGTH, WIDTH)
    return drawn.astype(jnp.bfloat16)


def draw_starts(key, part):
    picks = jax.random.randint(jax.random.fold_in(key, 21), (BATCH, SEQ_BLOCKS), 0, 8)
    drawn = (picks == 0).astype(jnp.int32)
    rows = lax.broadcasted_iota(jnp.int32, (BATCH, SEQ_BLOCKS), 0)
    columns = lax.broadcasted_iota(jnp.int32, (BATCH, SEQ_BLOCKS), 1)
    single = (columns == 0).astype(jnp.int32)
    return jnp.where(rows == 0, single, drawn)


def touch_ends(values, stream_key, low, high):
    longest = values.shape.index(max(values.shape))
    spots = []
    for shift in (0, 1):
        where = [jax.random.randint(jax.random.fold_in(stream_key, axis), (), 0, length) for axis, length in enumerate(values.shape)]
        where[longest] = (where[longest] + shift) % values.shape[longest]
        spots.append(tuple(where))
    return values.at[spots[0]].set(low).at[spots[1]].set(high)


def shard_levels(own_key, extent, cuts, least, top_value):
    gain = 1.0
    for axis_at, shards_of in cuts:
        draws = jax.random.uniform(jax.random.fold_in(jax.random.fold_in(own_key, 6), axis_at), (shards_of,), jnp.float32, least / len(cuts), top_value / len(cuts))
        gain = gain * jnp.repeat(jnp.exp(draws), extent[axis_at] // shards_of).reshape((-1,) + (1,) * (len(extent) - 1 - axis_at))
    return gain


def scatter_about(key, extent, scale, limit, cuts=(), held_as=jnp.bfloat16):
    entries = jax.random.normal(key, extent, jnp.float32) * scale
    if len(cuts) > 0:
        entries = shard_levels(key, extent, cuts, -0.22, 0.18) * entries
    return jnp.clip(entries, min=-limit, max=limit).astype(held_as)


def setup_inputs(seed: int = 0) -> dict:
    seeds = jax.random.split(jax.random.key(seed), 8)
    queries = draw_queries(jax.random.fold_in(seeds[7], 71), 0)
    keys = scatter_about(seeds[1], (BATCH, LENGTH, WIDTH), 4.0, 24.0, ((0, 4), (1, 32)))
    values = draw_values(jax.random.fold_in(seeds[7], 71), 0)
    codes = touch_ends(jax.random.randint(seeds[3], (BATCH, HEADS, LENGTH), 0, CODES), jax.random.fold_in(seeds[3], 1), 0, CODES - 1).astype(jnp.int32)
    starts = draw_starts(jax.random.fold_in(seeds[7], 71), 0)
    old_centroids = scatter_about(seeds[5], (HEADS, CODES, HEAD_DIM), 1.0, 6.0, (), jnp.float32)
    old_counts = jnp.clip(jnp.exp(jax.random.uniform(seeds[6], (HEADS, CODES), jnp.float32, math.log(4.0), math.log(64.0))), 4.0, 64.0)
    return {"queries": queries, "keys": keys, "values": values, "codes": codes, "starts": starts, "old_centroids": old_centroids, "old_counts": old_counts}


RETAIN = 0.9
NEGATIVE = -1e30


def one_hot_rows(code_block):
    return (code_block[:, :, None] == jnp.arange(CODES, dtype=jnp.int32)[None, None, :]).astype(jnp.bfloat16)


def rounded(array):
    return lax.optimization_barrier(array.astype(jnp.bfloat16)).astype(jnp.float32)


def refresh_codes(sums, counts, centroids, previous):
    return (RETAIN * previous[..., None] * centroids + (1.0 - RETAIN) * sums) / (RETAIN * previous + (1.0 - RETAIN) * counts)[..., None]


def reference(queries, keys, values, codes, starts, old_centroids, old_counts):
    code_blocks = codes.reshape(BATCH, HEADS, SEQ_BLOCKS, BLOCK).transpose(0, 2, 1, 3)
    flat_codes = code_blocks.reshape(BATCH * SEQ_BLOCKS, HEADS, BLOCK)
    flat_keys = keys.reshape(BATCH * SEQ_BLOCKS, BLOCK, HEADS, HEAD_DIM)

    def gather_stats(running, block_pair):
        hot_table = one_hot_rows(block_pair[0]).astype(jnp.float32)
        sums = running[0] + jnp.einsum('hts,thd->hsd', hot_table, block_pair[1].astype(jnp.float32))
        return (sums, running[1] + jnp.sum(hot_table, axis=1)), None

    zero_sums = jnp.zeros((HEADS, CODES, HEAD_DIM), jnp.float32)
    zero_counts = jnp.zeros((HEADS, CODES), jnp.float32)
    (key_sums, code_counts), ignored = lax.scan(gather_stats, (zero_sums, zero_counts), (flat_codes, flat_keys))
    codebook = refresh_codes(key_sums, code_counts, old_centroids, old_counts)
    codebook_half = rounded(codebook)
    score_scale = HEAD_DIM ** -0.5
    positions = jnp.arange(BLOCK, dtype=jnp.int32)
    causal = positions[:, None] >= positions[None, :]
    query_blocks = queries.reshape(BATCH, SEQ_BLOCKS, BLOCK, HEADS, HEAD_DIM)
    value_blocks = values.reshape(BATCH, SEQ_BLOCKS, BLOCK, HEADS, HEAD_DIM)

    def attend(running, inputs):
        query_part, value_part, code_part, start_flag = inputs
        survive = (1 - start_flag).astype(jnp.float32)
        cache_sums = survive * running[0]
        cache_counts = survive * running[1]
        hot_table = one_hot_rows(code_part).astype(jnp.float32)
        code_means = rounded(cache_sums / jnp.maximum(cache_counts, 1.0)[..., None])
        count_bias = jnp.where(cache_counts > 0, jnp.log(jnp.maximum(cache_counts, 1.0)), NEGATIVE)
        query_float = query_part.astype(jnp.float32)
        code_scores = jnp.einsum('thd,hsd->hts', query_float, codebook_half) * score_scale + count_bias[:, None, :]
        key_codes = rounded(jnp.einsum('hts,hsd->htd', hot_table, codebook_half))
        local_scores = jnp.where(causal[None], jnp.einsum('ihd,hjd->hij', query_float, key_codes) * score_scale, NEGATIVE)
        row_top = jnp.maximum(jnp.max(code_scores, axis=-1), jnp.max(local_scores, axis=-1))
        code_weights = jnp.exp(code_scores - row_top[..., None])
        local_weights = jnp.where(causal[None], jnp.exp(local_scores - row_top[..., None]), 0.0)
        denominator = jnp.sum(code_weights, axis=-1) + jnp.sum(local_weights, axis=-1)
        value_float = value_part.astype(jnp.float32)
        mixed_part = jnp.einsum('hts,hsd->htd', rounded(code_weights), code_means) + jnp.einsum('hij,jhd->hid', rounded(local_weights), value_float)
        out_rows = (mixed_part / denominator[..., None]).transpose(1, 0, 2).reshape(BLOCK, WIDTH).astype(jnp.bfloat16)
        block_sums = jnp.einsum('hts,thd->hsd', hot_table, value_float)
        block_counts = jnp.sum(hot_table, axis=1)
        return (cache_sums + block_sums, cache_counts + block_counts), out_rows

    def one_sequence(inputs):
        final_state, out_blocks = lax.scan(attend, (zero_sums, zero_counts), inputs)
        return out_blocks

    out_all = lax.map(one_sequence, (query_blocks, value_blocks, code_blocks, starts))
    mixed = out_all.reshape(BATCH, LENGTH, WIDTH)
    return (mixed, codebook)
```

```python
import functools

import jax
import jax.numpy as jnp
from jax import lax
from jax.experimental import pallas as pl
from jax.experimental.pallas import tpu as pltpu
from jax.sharding import PartitionSpec as P

HEADS = 16
HEAD_DIM = 128
CODES = 512
BLOCK = 512
TOK_DEV = 1024
RETAIN = 0.9
NEGATIVE = -1e30
SCORE_TO_LOG2 = 1.4426950408889634 * HEAD_DIM**-0.5

KEY_ROWS = 1032
VAL_ROWS = 264
CHIPS = 16
DPS = 4
F32 = jnp.float32
BF16 = jnp.bfloat16
MESH = pl.DeviceIdType.MESH


def column(row):
    return jnp.broadcast_to(row, (128, 128)).T


def head_row(ref, h, lanes, batched):
    tile = pl.ds(pl.multiple_of((h // 8) * 8, 8), 8)
    rows = ref[0, tile, lanes] if batched else ref[tile, lanes]
    picked = lax.broadcasted_iota(jnp.int32, rows.shape, 0) == h % 8
    return jnp.sum(jnp.where(picked, rows, jnp.zeros_like(rows)), axis=0, keepdims=True)


def stats_kernel(starts_ref, codes_ref, k_ref, v_ref, kin_ref, tail_ref, head_ref, first_ref):
    h = pl.program_id(0)
    f0 = starts_ref[0, 0].astype(F32)
    f1 = starts_ref[0, 1].astype(F32)
    s1 = 1.0 - f1
    code_iota = lax.broadcasted_iota(jnp.int32, (CODES, BLOCK), 0)
    lane = lax.broadcasted_iota(jnp.int32, (BLOCK, 128), 1).astype(F32)
    place = lax.broadcasted_iota(jnp.int32, (BLOCK, 128), 0).astype(F32)
    sums, counts = [], []
    for b in range(2):
        rows = slice(b * BLOCK, (b + 1) * BLOCK)
        code_row = head_row(codes_ref, h, rows, True)
        hot = jnp.where(code_iota == code_row, 1.0, 0.0).astype(BF16)
        pair = jnp.concatenate([k_ref[0, rows, :], v_ref[0, rows, :]], axis=1)
        sums.append(jnp.dot(hot, pair, preferred_element_type=F32))
        code_col = jnp.broadcast_to(code_row.astype(F32), (128, BLOCK)).T
        counted = []
        for r in range(4):
            same = code_col == lane + 128.0 * r
            counted.append(jnp.sum(jnp.where(same, 1.0, 0.0), axis=0, keepdims=True))
            first_ref[0, b : b + 1, r * 128 : (r + 1) * 128] = jnp.min(
                jnp.where(same, place, float(BLOCK)), axis=0, keepdims=True
            )
        counts.append(counted)
    first_ref[0, 2:8, :] = jnp.zeros((6, CODES), F32)
    key_sums = sums[0][:, :128] + sums[1][:, :128]
    key_counts = jnp.concatenate([counts[0][r] + counts[1][r] for r in range(4)], axis=0)

    @pl.when(h % 2 == 0)
    def _():
        kin_ref[0, 0:512, :] = key_sums
        kin_ref[0, 1024:1028, :] = key_counts

    @pl.when(h % 2 == 1)
    def _():
        kin_ref[0, 512:1024, :] = key_sums
        kin_ref[0, 1028:1032, :] = key_counts

    flag = jnp.broadcast_to(jnp.maximum(f0, f1), (1, 128))
    pad = jnp.zeros((5, 128), F32)
    for g in range(2):
        part = slice(g * 256, (g + 1) * 256)
        head_ref[g, 0:256, :] = sums[0][part, 128:]
        tail_ref[g, 0:256, :] = s1 * sums[0][part, 128:] + sums[1][part, 128:]
        early = [counts[0][2 * g], counts[0][2 * g + 1]]
        late = [s1 * counts[0][2 * g + i] + counts[1][2 * g + i] for i in range(2)]
        head_ref[g, 256:264, :] = jnp.concatenate(early + [flag, pad], axis=0)
        tail_ref[g, 256:264, :] = jnp.concatenate(late + [flag, pad], axis=0)


def statistics(starts, codes, keys, values):
    token = pl.BlockSpec((1, TOK_DEV, HEAD_DIM), lambda h: (0, 0, h))
    packed = pl.BlockSpec((2, VAL_ROWS, 128), lambda h: (h, 0, 0))
    return pl.pallas_call(
        stats_kernel,
        name="statistics",
        grid=(HEADS,),
        out_shape=(
            jax.ShapeDtypeStruct((8, KEY_ROWS, 128), F32),
            jax.ShapeDtypeStruct((32, VAL_ROWS, 128), F32),
            jax.ShapeDtypeStruct((32, VAL_ROWS, 128), F32),
            jax.ShapeDtypeStruct((HEADS, 8, CODES), F32),
        ),
        in_specs=[
            pl.BlockSpec(memory_space=pltpu.SMEM),
            pl.BlockSpec((1, HEADS, TOK_DEV), lambda h: (0, 0, 0)),
            token,
            token,
        ],
        out_specs=[
            pl.BlockSpec((1, KEY_ROWS, 128), lambda h: (h // 2, 0, 0)),
            packed,
            packed,
            pl.BlockSpec((1, 8, CODES), lambda h: (h, 0, 0)),
        ],
        compiler_params=pltpu.CompilerParams(vmem_limit_bytes=40 << 20),
    )(starts, codes, keys, values)


def exchange_kernel(
    kin, vin, kout, vout,
    k0, kchip, k1, s1, k2, own, v0, chip, v1, ent, v2, back,
    core_send, core_recv, dp_send, dp_recv, chip_send, chip_recv,
):
    y = lax.axis_index("dp")
    me = lax.axis_index("seq")
    c = me % 2
    p = me // 2
    other = {"seq": p * 2 + (1 - c)}

    def at_chip(j):
        return {"seq": j * 2 + c}

    def remote(src, dst, send, recv, device):
        return pltpu.make_async_remote_copy(
            src_ref=src, dst_ref=dst, send_sem=send, recv_sem=recv,
            device_id=device, device_id_type=MESH,
        )

    def others(count, mine, body):
        def step(k, carry):
            body(lax.rem(mine + k, count))
            return carry

        lax.fori_loop(1, count, step, 0)

    barrier = pltpu.get_barrier_semaphore()

    def greet(device):
        pl.semaphore_signal(barrier, inc=1, device_id=device, device_id_type=MESH)

    greet(other)
    others(CHIPS, p, lambda j: greet(at_chip(j)))
    others(DPS, y, lambda j: greet({"dp": j}))
    pl.semaphore_wait(barrier, 1 + (CHIPS - 1) + (DPS - 1))

    key_core = remote(kin.at[pl.ds(4 * (1 - c), 4)], k0, core_send.at[0], core_recv.at[0], other)
    val_core = remote(vin.at[pl.ds(16 * (1 - c), 16)], v0, core_send.at[1], core_recv.at[1], other)
    key_core.start()
    val_core.start()

    key_core.wait_recv()

    def add_core(q, carry):
        kchip[q] = kin[4 * c + q] + k0[q]
        return carry

    lax.fori_loop(0, 4, add_core, 0)

    def key_dp(j, slot, sem):
        return remote(kchip.at[j], k1.at[slot], dp_send.at[0, j], dp_recv.at[0, sem], {"dp": j})

    others(DPS, y, lambda j: key_dp(j, y, y).start())

    val_core.wait_recv()

    def join_cores(g, carry):
        mine = vin[16 * c + g]
        theirs = v0[g]
        early = jnp.where(c == 0, mine, theirs)
        late = jnp.where(c == 0, theirs, mine)
        chip[g] = late + (1.0 - late[258:259, :]) * early
        return carry

    lax.fori_loop(0, 16, join_cores, 0)

    def val_out(j, slot, sem):
        return remote(
            chip.at[j], v1.at[slot], chip_send.at[0, j], chip_recv.at[0, sem], at_chip(j)
        )

    others(CHIPS, p, lambda j: val_out(j, p, p).start())
    v1[p] = chip[p]

    k1[y] = kchip[y]
    others(DPS, y, lambda j: key_dp(j, j, j).wait_recv())
    tallied = (k1[0, 1024:1032, :] + k1[1, 1024:1032, :]) + (k1[2, 1024:1032, :] + k1[3, 1024:1032, :])

    def add_dp(j, carry):
        rows = pl.ds(pl.multiple_of(j * 64, 64), 64)
        s1[j, 0:64, :] = (k1[0, rows, :] + k1[1, rows, :]) + (k1[2, rows, :] + k1[3, rows, :])
        s1[j, 64:72, :] = tallied
        return carry

    lax.fori_loop(0, CHIPS, add_dp, 0)

    def key_out(j, slot, sem):
        return remote(s1.at[j], k2.at[slot], chip_send.at[1, j], chip_recv.at[1, sem], at_chip(j))

    others(CHIPS, p, lambda j: key_out(j, p, p).start())
    k2[p] = s1[p]

    others(CHIPS, p, lambda j: val_out(j, j, j).wait_recv())

    def scan(j, run):
        ent[j] = run
        part = v1[j]
        return part + (1.0 - part[258:259, :]) * run

    lax.fori_loop(0, CHIPS, scan, jnp.zeros((VAL_ROWS, 128), F32))

    others(CHIPS, p, lambda j: key_out(j, j, j).wait_recv())
    total = lax.fori_loop(0, CHIPS, lambda j, run: run + k2[j], jnp.zeros((72, 128), F32))
    own[...] = total[0:64]
    quarter = 4 * c + y
    mine = pl.ds(pl.multiple_of(p * 64, 64), 64)
    kout[quarter, mine, :] = total[0:64]
    kout[quarter, 1024:1032, :] = total[64:72]

    def key_back(j, slot, sem):
        rows = pl.ds(pl.multiple_of(slot * 64, 64), 64)
        return remote(
            own, kout.at[quarter, rows], chip_send.at[2, j], chip_recv.at[2, sem], at_chip(j)
        )

    others(CHIPS, p, lambda j: key_back(j, p, p).start())

    def val_back(j, slot, sem):
        return remote(
            ent.at[j], v2.at[slot], chip_send.at[3, j], chip_recv.at[3, sem], at_chip(j)
        )

    others(CHIPS, p, lambda j: val_back(j, p, p).start())
    v2[p] = ent[p]

    others(CHIPS, p, lambda j: key_back(j, j, j).wait_recv())

    def key_spread(j, held, sem):
        part = kout.at[4 * c + held]
        return remote(part, part, dp_send.at[1, j], dp_recv.at[1, sem], {"dp": j})

    def key_share(held, half):
        part = kout.at[4 * half + held]
        return remote(part, part, core_send.at[3 + held], core_recv.at[3 + held], other)

    others(DPS, y, lambda j: key_spread(j, y, y).start())
    key_share(y, c).start()

    def pass_on(j):
        key_spread(j, j, j).wait_recv()
        key_share(j, c).start()

    others(DPS, y, pass_on)

    others(CHIPS, p, lambda j: val_back(j, j, j).wait_recv())

    def split_cores(g, carry):
        early = jnp.where(c == 0, vin[16 * c + g], v0[g])
        first = v2[g]
        second = early + (1.0 - early[258:259, :]) * first
        vout[16 * c + g] = jnp.where(c == 0, first, second)
        back[g] = jnp.where(c == 0, second, first)
        return carry

    lax.fori_loop(0, 16, split_cores, 0)
    half = vout.at[pl.ds(16 * c, 16)]
    val_core_back = remote(back, half, core_send.at[2], core_recv.at[2], other)
    val_core_back.start()

    def finish(held, carry):
        key_share(held, 1 - c).wait_recv()
        return carry

    lax.fori_loop(0, DPS, finish, 0)
    remote(
        back, vout.at[pl.ds(16 * (1 - c), 16)], core_send.at[2], core_recv.at[2], other
    ).wait_recv()

    key_core.wait_send()
    val_core.wait_send()
    val_core_back.wait_send()

    def sent_dp(j):
        key_dp(j, j, j).wait_send()
        key_spread(j, y, j).wait_send()

    others(DPS, y, sent_dp)

    def sent_core(held, carry):
        key_share(held, c).wait_send()
        return carry

    lax.fori_loop(0, DPS, sent_core, 0)

    def sent_chip(j):
        val_out(j, j, j).wait_send()
        key_out(j, j, j).wait_send()
        key_back(j, j, j).wait_send()
        val_back(j, j, j).wait_send()

    others(CHIPS, p, sent_chip)


def exchange(kin, vin):
    whole = pl.BlockSpec(memory_space=pltpu.VMEM)
    return pl.pallas_call(
        exchange_kernel,
        name="exchange",
        out_shape=(
            jax.ShapeDtypeStruct((8, KEY_ROWS, 128), F32),
            jax.ShapeDtypeStruct((32, VAL_ROWS, 128), F32),
        ),
        in_specs=[whole, whole],
        out_specs=[whole, whole],
        scratch_shapes=[
            pltpu.VMEM((4, KEY_ROWS, 128), F32),
            pltpu.VMEM((4, KEY_ROWS, 128), F32),
            pltpu.VMEM((4, KEY_ROWS, 128), F32),
            pltpu.VMEM((CHIPS, 72, 128), F32),
            pltpu.VMEM((CHIPS, 72, 128), F32),
            pltpu.VMEM((64, 128), F32),
            pltpu.VMEM((16, VAL_ROWS, 128), F32),
            pltpu.VMEM((16, VAL_ROWS, 128), F32),
            pltpu.VMEM((CHIPS, VAL_ROWS, 128), F32),
            pltpu.VMEM((CHIPS, VAL_ROWS, 128), F32),
            pltpu.VMEM((CHIPS, VAL_ROWS, 128), F32),
            pltpu.VMEM((16, VAL_ROWS, 128), F32),
            pltpu.SemaphoreType.DMA((7,)),
            pltpu.SemaphoreType.DMA((7,)),
            pltpu.SemaphoreType.DMA((2, DPS)),
            pltpu.SemaphoreType.DMA((2, DPS)),
            pltpu.SemaphoreType.DMA((4, CHIPS)),
            pltpu.SemaphoreType.DMA((4, CHIPS)),
        ],
        compiler_params=pltpu.CompilerParams(
            collective_id=0, has_side_effects=True, vmem_limit_bytes=56 << 20
        ),
    )(kin, vin)


def attend_kernel(
    starts_ref, codes_ref, q_ref, v_ref, keys_ref, enter_ref, head_ref, first_ref,
    cent_ref, old_ref, out_ref, book_out_ref, book_ref,
):
    h = pl.program_id(0)
    odd = h % 2
    alive = [1.0 - starts_ref[0, b].astype(F32) for b in range(2)]

    tallied = keys_ref[0, 1024:1032, :]
    tallied = jnp.where(odd == 0, tallied[0:4], tallied[4:8])
    for r in range(4):
        rows = slice(r * 128, (r + 1) * 128)
        old = column(head_row(old_ref, h, rows, False))
        now = column(tallied[r : r + 1])
        sums = keys_ref[0, pl.ds(pl.multiple_of(odd * 512 + r * 128, 128), 128), :]
        book_ref[rows, :] = (RETAIN * old * cent_ref[0, rows, :] + (1.0 - RETAIN) * sums) / (
            RETAIN * old + (1.0 - RETAIN) * now
        )
    share = pl.multiple_of(lax.axis_index("dp") * 128, 128)
    book_out_ref[0] = book_ref[pl.ds(share, 128), :]
    book = book_ref[...].astype(BF16)

    def unpacked(ref):
        sums = jnp.concatenate([ref[0, 0:256, :], ref[1, 0:256, :]], axis=0)
        counts = jnp.concatenate(
            [ref[0, 256:257, :], ref[0, 257:258, :], ref[1, 256:257, :], ref[1, 257:258, :]],
            axis=1,
        )
        return sums, counts

    sums, counts = unpacked(enter_ref)
    code_iota = lax.broadcasted_iota(jnp.int32, (CODES, BLOCK), 0)
    square_row = lax.broadcasted_iota(jnp.int32, (128, 128), 0)
    ones_column = jnp.where(
        lax.broadcasted_iota(jnp.int32, (BLOCK, 128), 1) == 0, 1.0, 0.0
    ).astype(BF16)
    half = BLOCK // 2
    causal = lax.broadcasted_iota(jnp.int32, (half, half), 0) >= lax.broadcasted_iota(
        jnp.int32, (half, half), 1
    )
    place = lax.broadcasted_iota(jnp.int32, (half, CODES), 0).astype(F32)
    for b in range(2):
        if b == 1:
            more, added = unpacked(head_ref)
            sums, counts = sums + more, counts + added
        sums, counts = alive[b] * sums, alive[b] * counts
        present = counts > 0
        bias = jnp.where(present, jnp.log2(jnp.maximum(counts, 1.0)), 0.0)
        opens = jnp.where(present, -1.0, first_ref[0, b : b + 1, :])
        high = jnp.floor(counts * (1.0 / 256.0)) * 256.0
        low = counts - high
        columns = []
        for r in range(4):
            lanes = slice(r * 128, (r + 1) * 128)
            columns.append(
                jnp.where(
                    square_row == 0, high[:, lanes], jnp.where(square_row == 1, low[:, lanes], 0.0)
                ).T
            )
        cache = jnp.concatenate([sums, jnp.concatenate(columns, axis=0)], axis=1).astype(BF16)
        rows = slice(b * BLOCK, (b + 1) * BLOCK)
        code_row = head_row(codes_ref, h, rows, True)
        hot = jnp.where(code_iota == code_row, 1.0, 0.0).astype(BF16)
        local = jnp.concatenate([v_ref[0, rows, :], ones_column], axis=1)
        for i in range(2):
            at = slice(b * BLOCK + i * half, b * BLOCK + (i + 1) * half)
            scores = lax.dot_general(
                q_ref[0, at, :], book, (((1,), (1,)), ((), ())), preferred_element_type=F32
            )
            scores = scores * SCORE_TO_LOG2
            top = jnp.max(
                jnp.where(opens <= place + float(i * half), scores + bias, NEGATIVE),
                axis=1,
                keepdims=True,
            )
            weight = jnp.exp2(jnp.minimum(scores - top, 0.0)).astype(BF16)
            acc = jnp.dot(weight, cache, preferred_element_type=F32)
            if i == 1:
                early = jnp.dot(weight, hot[:, :half], preferred_element_type=F32).astype(BF16)
                acc = acc + jnp.dot(early, local[:half], preferred_element_type=F32)
            near = jnp.dot(weight, hot[:, i * half : (i + 1) * half], preferred_element_type=F32)
            near = jnp.where(causal, near, 0.0).astype(BF16)
            acc = acc + jnp.dot(
                near, local[i * half : (i + 1) * half], preferred_element_type=F32
            )
            out_ref[0, at, :] = (acc[:, :128] / (acc[:, 128:129] + acc[:, 129:130])).astype(BF16)


def attend(starts, codes, queries, values, keys, enter, head, first, centroids, old):
    token = pl.BlockSpec((1, TOK_DEV, HEAD_DIM), lambda h: (0, 0, h))
    packed = pl.BlockSpec((2, VAL_ROWS, 128), lambda h: (h, 0, 0))
    return pl.pallas_call(
        attend_kernel,
        name="attend",
        grid=(HEADS,),
        out_shape=(
            jax.ShapeDtypeStruct((1, TOK_DEV, HEADS * HEAD_DIM), BF16),
            jax.ShapeDtypeStruct((HEADS, CODES // DPS, HEAD_DIM), F32),
        ),
        in_specs=[
            pl.BlockSpec(memory_space=pltpu.SMEM),
            pl.BlockSpec((1, HEADS, TOK_DEV), lambda h: (0, 0, 0)),
            token,
            token,
            pl.BlockSpec((1, KEY_ROWS, 128), lambda h: (h // 2, 0, 0)),
            packed,
            packed,
            pl.BlockSpec((1, 8, CODES), lambda h: (h, 0, 0)),
            pl.BlockSpec((1, CODES, HEAD_DIM), lambda h: (h, 0, 0)),
            pl.BlockSpec((HEADS, CODES), lambda h: (0, 0)),
        ],
        out_specs=[token, pl.BlockSpec((1, CODES // DPS, HEAD_DIM), lambda h: (h, 0, 0))],
        scratch_shapes=[pltpu.VMEM((CODES, HEAD_DIM), F32)],
        compiler_params=pltpu.CompilerParams(vmem_limit_bytes=40 << 20),
    )(starts, codes, queries, values, keys, enter, head, first, centroids, old)


def shards(queries, keys, values, codes, starts, old_centroids, old_counts):
    kin, tail, head, first = statistics(starts, codes, keys, values)
    total, enter = exchange(kin, tail)
    return attend(
        starts, codes, queries, values, total, enter, head, first, old_centroids, old_counts
    )


def solution(mesh):
    placed = (
        P("dp", "seq", None),
        P("dp", "seq", None),
        P("dp", "seq", None),
        P("dp", None, "seq"),
        P("dp", "seq"),
        P(),
        P(),
    )
    return jax.shard_map(
        shards,
        mesh=mesh,
        in_specs=placed,
        out_specs=(P("dp", "seq", None), P(None, "dp", None)),
        check_vma=False,
    )
```

```python
import functools

import jax
import jax.numpy as jnp
from jax import lax
from jax.experimental import pallas as pl
from jax.experimental.pallas import tpu as pltpu
from jax.sharding import PartitionSpec as P

HEADS = 16
HEAD_DIM = 128
CODES = 512
BLOCK = 512
TOK_DEV = 1024
RETAIN = 0.9
NEGATIVE = -1e30
SCORE_TO_LOG2 = 1.4426950408889634 * HEAD_DIM**-0.5

KEY_ROWS = 1032
VAL_ROWS = 264
CHIPS = 16
DPS = 4
F32 = jnp.float32
BF16 = jnp.bfloat16
MESH = pl.DeviceIdType.MESH


def column(row):
    return jnp.broadcast_to(row, (128, 128)).T


def head_row(ref, h, lanes, batched):
    tile = pl.ds(pl.multiple_of((h // 8) * 8, 8), 8)
    rows = ref[0, tile, lanes] if batched else ref[tile, lanes]
    picked = lax.broadcasted_iota(jnp.int32, rows.shape, 0) == h % 8
    return jnp.sum(jnp.where(picked, rows, jnp.zeros_like(rows)), axis=0, keepdims=True)


def stats_kernel(starts_ref, codes_ref, k_ref, v_ref, kin_ref, tail_ref, head_ref, first_ref):
    h = pl.program_id(0)
    f0 = starts_ref[0, 0].astype(F32)
    f1 = starts_ref[0, 1].astype(F32)
    s1 = 1.0 - f1
    code_iota = lax.broadcasted_iota(jnp.int32, (CODES, BLOCK), 0)
    lane = lax.broadcasted_iota(jnp.int32, (BLOCK, 128), 1).astype(F32)
    place = lax.broadcasted_iota(jnp.int32, (BLOCK, 128), 0).astype(F32)
    sums, counts = [], []
    for b in range(2):
        rows = slice(b * BLOCK, (b + 1) * BLOCK)
        code_row = head_row(codes_ref, h, rows, True)
        hot = jnp.where(code_iota == code_row, 1.0, 0.0).astype(BF16)
        pair = jnp.concatenate([k_ref[0, rows, :], v_ref[0, rows, :]], axis=1)
        sums.append(jnp.dot(hot, pair, preferred_element_type=F32))
        code_col = jnp.broadcast_to(code_row.astype(F32), (128, BLOCK)).T
        counted = []
        for r in range(4):
            same = code_col == lane + 128.0 * r
            counted.append(jnp.sum(jnp.where(same, 1.0, 0.0), axis=0, keepdims=True))
            first_ref[0, b : b + 1, r * 128 : (r + 1) * 128] = jnp.min(
                jnp.where(same, place, float(BLOCK)), axis=0, keepdims=True
            )
        counts.append(counted)
    first_ref[0, 2:8, :] = jnp.zeros((6, CODES), F32)
    key_sums = sums[0][:, :128] + sums[1][:, :128]
    key_counts = jnp.concatenate([counts[0][r] + counts[1][r] for r in range(4)], axis=0)

    @pl.when(h % 2 == 0)
    def _():
        kin_ref[0, 0:512, :] = key_sums
        kin_ref[0, 1024:1028, :] = key_counts

    @pl.when(h % 2 == 1)
    def _():
        kin_ref[0, 512:1024, :] = key_sums
        kin_ref[0, 1028:1032, :] = key_counts

    flag = jnp.broadcast_to(jnp.maximum(f0, f1), (1, 128))
    pad = jnp.zeros((5, 128), F32)
    for g in range(2):
        part = slice(g * 256, (g + 1) * 256)
        head_ref[g, 0:256, :] = sums[0][part, 128:]
        tail_ref[g, 0:256, :] = s1 * sums[0][part, 128:] + sums[1][part, 128:]
        early = [counts[0][2 * g], counts[0][2 * g + 1]]
        late = [s1 * counts[0][2 * g + i] + counts[1][2 * g + i] for i in range(2)]
        head_ref[g, 256:264, :] = jnp.concatenate(early + [flag, pad], axis=0)
        tail_ref[g, 256:264, :] = jnp.concatenate(late + [flag, pad], axis=0)


def statistics(starts, codes, keys, values):
    token = pl.BlockSpec((1, TOK_DEV, HEAD_DIM), lambda h: (0, 0, h))
    packed = pl.BlockSpec((2, VAL_ROWS, 128), lambda h: (h, 0, 0))
    return pl.pallas_call(
        stats_kernel,
        name="statistics",
        grid=(HEADS,),
        out_shape=(
            jax.ShapeDtypeStruct((8, KEY_ROWS, 128), F32),
            jax.ShapeDtypeStruct((32, VAL_ROWS, 128), F32),
            jax.ShapeDtypeStruct((32, VAL_ROWS, 128), F32),
            jax.ShapeDtypeStruct((HEADS, 8, CODES), F32),
        ),
        in_specs=[
            pl.BlockSpec(memory_space=pltpu.SMEM),
            pl.BlockSpec((1, HEADS, TOK_DEV), lambda h: (0, 0, 0)),
            token,
            token,
        ],
        out_specs=[
            pl.BlockSpec((1, KEY_ROWS, 128), lambda h: (h // 2, 0, 0)),
            packed,
            packed,
            pl.BlockSpec((1, 8, CODES), lambda h: (h, 0, 0)),
        ],
        compiler_params=pltpu.CompilerParams(vmem_limit_bytes=60 << 20),
    )(starts, codes, keys, values)


def exchange_kernel(
    kin, vin, kout, vout,
    k0, kchip, k1, s1, k2, own, v0, chip, v1, ent, v2, back,
    core_send, core_recv, dp_send, dp_recv, chip_send, chip_recv,
):
    y = lax.axis_index("dp")
    me = lax.axis_index("seq")
    c = me % 2
    p = me // 2
    other = {"seq": p * 2 + (1 - c)}

    def at_chip(j):
        return {"seq": j * 2 + c}

    def remote(src, dst, send, recv, device):
        return pltpu.make_async_remote_copy(
            src_ref=src, dst_ref=dst, send_sem=send, recv_sem=recv,
            device_id=device, device_id_type=MESH,
        )

    def others(count, mine, body):
        def step(k, carry):
            body(lax.rem(mine + k, count))
            return carry

        lax.fori_loop(1, count, step, 0)

    barrier = pltpu.get_barrier_semaphore()

    def greet(device):
        pl.semaphore_signal(barrier, inc=1, device_id=device, device_id_type=MESH)

    greet(other)
    others(CHIPS, p, lambda j: greet(at_chip(j)))
    others(DPS, y, lambda j: greet({"dp": j}))
    pl.semaphore_wait(barrier, 1 + (CHIPS - 1) + (DPS - 1))

    key_core = remote(kin.at[pl.ds(4 * (1 - c), 4)], k0, core_send.at[0], core_recv.at[0], other)
    val_core = remote(vin.at[pl.ds(16 * (1 - c), 16)], v0, core_send.at[1], core_recv.at[1], other)
    key_core.start()
    val_core.start()

    key_core.wait_recv()

    def add_core(q, carry):
        kchip[q] = kin[4 * c + q] + k0[q]
        return carry

    lax.fori_loop(0, 4, add_core, 0)

    def key_dp(j, slot, sem):
        return remote(kchip.at[j], k1.at[slot], dp_send.at[0, j], dp_recv.at[0, sem], {"dp": j})

    others(DPS, y, lambda j: key_dp(j, y, y).start())

    val_core.wait_recv()

    def join_cores(g, carry):
        mine = vin[16 * c + g]
        theirs = v0[g]
        early = jnp.where(c == 0, mine, theirs)
        late = jnp.where(c == 0, theirs, mine)
        chip[g] = late + (1.0 - late[258:259, :]) * early
        return carry

    lax.fori_loop(0, 16, join_cores, 0)

    def val_out(j, slot, sem):
        return remote(
            chip.at[j], v1.at[slot], chip_send.at[0, j], chip_recv.at[0, sem], at_chip(j)
        )

    others(CHIPS, p, lambda j: val_out(j, p, p).start())
    v1[p] = chip[p]

    k1[y] = kchip[y]
    others(DPS, y, lambda j: key_dp(j, j, j).wait_recv())
    tallied = (k1[0, 1024:1032, :] + k1[1, 1024:1032, :]) + (k1[2, 1024:1032, :] + k1[3, 1024:1032, :])

    def add_dp(j, carry):
        rows = pl.ds(pl.multiple_of(j * 64, 64), 64)
        s1[j, 0:64, :] = (k1[0, rows, :] + k1[1, rows, :]) + (k1[2, rows, :] + k1[3, rows, :])
        s1[j, 64:72, :] = tallied
        return carry

    lax.fori_loop(0, CHIPS, add_dp, 0)

    def key_out(j, slot, sem):
        return remote(s1.at[j], k2.at[slot], chip_send.at[1, j], chip_recv.at[1, sem], at_chip(j))

    others(CHIPS, p, lambda j: key_out(j, p, p).start())
    k2[p] = s1[p]

    others(CHIPS, p, lambda j: val_out(j, j, j).wait_recv())

    def scan(j, run):
        ent[j] = run
        part = v1[j]
        return part + (1.0 - part[258:259, :]) * run

    lax.fori_loop(0, CHIPS, scan, jnp.zeros((VAL_ROWS, 128), F32))

    others(CHIPS, p, lambda j: key_out(j, j, j).wait_recv())
    total = lax.fori_loop(0, CHIPS, lambda j, run: run + k2[j], jnp.zeros((72, 128), F32))
    own[...] = total[0:64]
    quarter = 4 * c + y
    mine = pl.ds(pl.multiple_of(p * 64, 64), 64)
    kout[quarter, mine, :] = total[0:64]
    kout[quarter, 1024:1032, :] = total[64:72]

    def key_back(j, slot, sem):
        rows = pl.ds(pl.multiple_of(slot * 64, 64), 64)
        return remote(
            own, kout.at[quarter, rows], chip_send.at[2, j], chip_recv.at[2, sem], at_chip(j)
        )

    others(CHIPS, p, lambda j: key_back(j, p, p).start())

    def val_back(j, slot, sem):
        return remote(
            ent.at[j], v2.at[slot], chip_send.at[3, j], chip_recv.at[3, sem], at_chip(j)
        )

    others(CHIPS, p, lambda j: val_back(j, p, p).start())
    v2[p] = ent[p]

    others(CHIPS, p, lambda j: key_back(j, j, j).wait_recv())

    def key_spread(j, held, sem):
        part = kout.at[4 * c + held]
        return remote(part, part, dp_send.at[1, j], dp_recv.at[1, sem], {"dp": j})

    def key_share(held, half):
        part = kout.at[4 * half + held]
        return remote(part, part, core_send.at[3 + held], core_recv.at[3 + held], other)

    others(DPS, y, lambda j: key_spread(j, y, y).start())
    key_share(y, c).start()

    def pass_on(j):
        key_spread(j, j, j).wait_recv()
        key_share(j, c).start()

    others(DPS, y, pass_on)

    others(CHIPS, p, lambda j: val_back(j, j, j).wait_recv())

    def split_cores(g, carry):
        early = jnp.where(c == 0, vin[16 * c + g], v0[g])
        first = v2[g]
        second = early + (1.0 - early[258:259, :]) * first
        vout[16 * c + g] = jnp.where(c == 0, first, second)
        back[g] = jnp.where(c == 0, second, first)
        return carry

    lax.fori_loop(0, 16, split_cores, 0)
    half = vout.at[pl.ds(16 * c, 16)]
    val_core_back = remote(back, half, core_send.at[2], core_recv.at[2], other)
    val_core_back.start()

    def finish(held, carry):
        key_share(held, 1 - c).wait_recv()
        return carry

    lax.fori_loop(0, DPS, finish, 0)
    remote(
        back, vout.at[pl.ds(16 * (1 - c), 16)], core_send.at[2], core_recv.at[2], other
    ).wait_recv()

    key_core.wait_send()
    val_core.wait_send()
    val_core_back.wait_send()

    def sent_dp(j):
        key_dp(j, j, j).wait_send()
        key_spread(j, y, j).wait_send()

    others(DPS, y, sent_dp)

    def sent_core(held, carry):
        key_share(held, c).wait_send()
        return carry

    lax.fori_loop(0, DPS, sent_core, 0)

    def sent_chip(j):
        val_out(j, j, j).wait_send()
        key_out(j, j, j).wait_send()
        key_back(j, j, j).wait_send()
        val_back(j, j, j).wait_send()

    others(CHIPS, p, sent_chip)


def exchange(kin, vin):
    whole = pl.BlockSpec(memory_space=pltpu.VMEM)
    return pl.pallas_call(
        exchange_kernel,
        name="exchange",
        out_shape=(
            jax.ShapeDtypeStruct((8, KEY_ROWS, 128), F32),
            jax.ShapeDtypeStruct((32, VAL_ROWS, 128), F32),
        ),
        in_specs=[whole, whole],
        out_specs=[whole, whole],
        scratch_shapes=[
            pltpu.VMEM((4, KEY_ROWS, 128), F32),
            pltpu.VMEM((4, KEY_ROWS, 128), F32),
            pltpu.VMEM((4, KEY_ROWS, 128), F32),
            pltpu.VMEM((CHIPS, 72, 128), F32),
            pltpu.VMEM((CHIPS, 72, 128), F32),
            pltpu.VMEM((64, 128), F32),
            pltpu.VMEM((16, VAL_ROWS, 128), F32),
            pltpu.VMEM((16, VAL_ROWS, 128), F32),
            pltpu.VMEM((CHIPS, VAL_ROWS, 128), F32),
            pltpu.VMEM((CHIPS, VAL_ROWS, 128), F32),
            pltpu.VMEM((CHIPS, VAL_ROWS, 128), F32),
            pltpu.VMEM((16, VAL_ROWS, 128), F32),
            pltpu.SemaphoreType.DMA((7,)),
            pltpu.SemaphoreType.DMA((7,)),
            pltpu.SemaphoreType.DMA((2, DPS)),
            pltpu.SemaphoreType.DMA((2, DPS)),
            pltpu.SemaphoreType.DMA((4, CHIPS)),
            pltpu.SemaphoreType.DMA((4, CHIPS)),
        ],
        compiler_params=pltpu.CompilerParams(
            collective_id=0, has_side_effects=True, vmem_limit_bytes=56 << 20
        ),
    )(kin, vin)


def attend_kernel(
    starts_ref, codes_ref, q_ref, v_ref, keys_ref, enter_ref, head_ref, first_ref,
    cent_ref, old_ref, out_ref, book_out_ref, book_ref,
):
    h = pl.program_id(0)
    odd = h % 2
    alive = [1.0 - starts_ref[0, b].astype(F32) for b in range(2)]

    tallied = keys_ref[0, 1024:1032, :]
    tallied = jnp.where(odd == 0, tallied[0:4], tallied[4:8])
    for r in range(4):
        rows = slice(r * 128, (r + 1) * 128)
        old = column(head_row(old_ref, h, rows, False))
        now = column(tallied[r : r + 1])
        sums = keys_ref[0, pl.ds(pl.multiple_of(odd * 512 + r * 128, 128), 128), :]
        book_ref[rows, :] = (RETAIN * old * cent_ref[0, rows, :] + (1.0 - RETAIN) * sums) / (
            RETAIN * old + (1.0 - RETAIN) * now
        )
    share = pl.multiple_of(lax.axis_index("dp") * 128, 128)
    book_out_ref[0] = book_ref[pl.ds(share, 128), :]
    book = book_ref[...].astype(BF16)

    def unpacked(ref):
        sums = jnp.concatenate([ref[0, 0:256, :], ref[1, 0:256, :]], axis=0)
        counts = jnp.concatenate(
            [ref[0, 256:257, :], ref[0, 257:258, :], ref[1, 256:257, :], ref[1, 257:258, :]],
            axis=1,
        )
        return sums, counts

    sums, counts = unpacked(enter_ref)
    code_iota = lax.broadcasted_iota(jnp.int32, (CODES, BLOCK), 0)
    square_row = lax.broadcasted_iota(jnp.int32, (128, 128), 0)
    ones_column = jnp.where(
        lax.broadcasted_iota(jnp.int32, (BLOCK, 128), 1) == 0, 1.0, 0.0
    ).astype(BF16)
    half = BLOCK // 2
    causal = lax.broadcasted_iota(jnp.int32, (BLOCK, half), 0) >= lax.broadcasted_iota(
        jnp.int32, (BLOCK, half), 1
    )
    place = lax.broadcasted_iota(jnp.int32, (BLOCK, CODES), 0).astype(F32)
    scores_all = lax.dot_general(
        q_ref[0], book, (((1,), (1,)), ((), ())), preferred_element_type=F32
    )
    for b in range(2):
        if b == 1:
            more, added = unpacked(head_ref)
            sums, counts = sums + more, counts + added
        sums, counts = alive[b] * sums, alive[b] * counts
        present = counts > 0
        bias = jnp.where(present, jnp.log2(jnp.maximum(counts, 1.0)), 0.0)
        opens = jnp.where(present, -1.0, first_ref[0, b : b + 1, :])
        high = jnp.floor(counts * (1.0 / 256.0)) * 256.0
        low = counts - high
        columns = []
        for r in range(4):
            lanes = slice(r * 128, (r + 1) * 128)
            columns.append(
                jnp.where(
                    square_row == 0, high[:, lanes], jnp.where(square_row == 1, low[:, lanes], 0.0)
                ).T
            )
        cache = jnp.concatenate([sums, jnp.concatenate(columns, axis=0)], axis=1).astype(BF16)
        rows = slice(b * BLOCK, (b + 1) * BLOCK)
        code_row = head_row(codes_ref, h, rows, True)
        hot = jnp.where(code_iota == code_row, 1.0, 0.0).astype(BF16)
        local = jnp.concatenate([v_ref[0, rows, :], ones_column], axis=1)
        scores = scores_all[b * BLOCK : (b + 1) * BLOCK] * SCORE_TO_LOG2
        top = jnp.max(
            jnp.where(opens <= place, scores + bias, NEGATIVE), axis=1, keepdims=True
        )
        weight = jnp.exp2(jnp.minimum(scores - top, 0.0)).astype(BF16)
        near = jnp.dot(weight, hot[:, :half], preferred_element_type=F32)
        near = jnp.where(causal, near, 0.0).astype(BF16)
        far = jnp.dot(weight[half:], hot[:, half:], preferred_element_type=F32)
        far = jnp.where(causal[:half], far, 0.0).astype(BF16)
        acc = jnp.dot(weight, cache, preferred_element_type=F32)
        acc = acc + jnp.dot(near, local[:half], preferred_element_type=F32)
        acc_far = acc[half:] + jnp.dot(far, local[half:], preferred_element_type=F32)
        top_rows = slice(b * BLOCK, b * BLOCK + half)
        low_rows = slice(b * BLOCK + half, (b + 1) * BLOCK)
        acc = acc[:half]
        out_ref[0, top_rows, :] = (acc[:, :128] / (acc[:, 128:129] + acc[:, 129:130])).astype(BF16)
        out_ref[0, low_rows, :] = (
            acc_far[:, :128] / (acc_far[:, 128:129] + acc_far[:, 129:130])
        ).astype(BF16)


def attend(starts, codes, queries, values, keys, enter, head, first, centroids, old):
    token = pl.BlockSpec((1, TOK_DEV, HEAD_DIM), lambda h: (0, 0, h))
    packed = pl.BlockSpec((2, VAL_ROWS, 128), lambda h: (h, 0, 0))
    return pl.pallas_call(
        attend_kernel,
        name="attend",
        grid=(HEADS,),
        out_shape=(
            jax.ShapeDtypeStruct((1, TOK_DEV, HEADS * HEAD_DIM), BF16),
            jax.ShapeDtypeStruct((HEADS, CODES // DPS, HEAD_DIM), F32),
        ),
        in_specs=[
            pl.BlockSpec(memory_space=pltpu.SMEM),
            pl.BlockSpec((1, HEADS, TOK_DEV), lambda h: (0, 0, 0)),
            token,
            token,
            pl.BlockSpec((1, KEY_ROWS, 128), lambda h: (h // 2, 0, 0)),
            packed,
            packed,
            pl.BlockSpec((1, 8, CODES), lambda h: (h, 0, 0)),
            pl.BlockSpec((1, CODES, HEAD_DIM), lambda h: (h, 0, 0)),
            pl.BlockSpec((HEADS, CODES), lambda h: (0, 0)),
        ],
        out_specs=[token, pl.BlockSpec((1, CODES // DPS, HEAD_DIM), lambda h: (h, 0, 0))],
        scratch_shapes=[pltpu.VMEM((CODES, HEAD_DIM), F32)],
        compiler_params=pltpu.CompilerParams(vmem_limit_bytes=60 << 20),
    )(starts, codes, queries, values, keys, enter, head, first, centroids, old)


def shards(queries, keys, values, codes, starts, old_centroids, old_counts):
    kin, tail, head, first = statistics(starts, codes, keys, values)
    total, enter = exchange(kin, tail)
    return attend(
        starts, codes, queries, values, total, enter, head, first, old_centroids, old_counts
    )


def solution(mesh):
    placed = (
        P("dp", "seq", None),
        P("dp", "seq", None),
        P("dp", "seq", None),
        P("dp", None, "seq"),
        P("dp", "seq"),
        P(),
        P(),
    )
    return jax.shard_map(
        shards,
        mesh=mesh,
        in_specs=placed,
        out_specs=(P("dp", "seq", None), P(None, "dp", None)),
        check_vma=False,
    )
```

```python
import jax
import jax.numpy as jnp
from jax import lax
from jax.experimental import pallas as pl
from jax.experimental.pallas import tpu as pltpu
from jax.sharding import PartitionSpec as P

HEADS = 16
HEAD_DIM = 128
CODES = 512
BLOCK = 512
TOK_DEV = 1024
RETAIN = 0.9
NEGATIVE = -1e30
SCORE_TO_LOG2 = 1.4426950408889634 * HEAD_DIM**-0.5

UNIT = 264
GROUPS = 4
F32 = jnp.float32
BF16 = jnp.bfloat16
MESH = pl.DeviceIdType.MESH

(KEY_CORE, VAL_CORE, KEY_Y, VAL_X, KEY_Z, VAL_Z, KEY_X, VAL_BACK, KEY_ZB, KEY_YB, KEY_CB, VAL_CB) = range(12)
PHASES = 12

ATTEND = 25
AT_JOIN = (6, 4)
AT_Y = (14, 3)
AT_SCAN = (14, 3)
AT_Z = (16, 3)
AT_ROWS = (16, 3)
AT_X = (18, 3)
AT_ZB = (20, 3)
AT_SPLIT = (22, 4)
AT_YB = (24, 4)


def column(row):
    return jnp.broadcast_to(row, (128, 128)).T


def head_row(ref, h, lanes, batched):
    tile = pl.ds(pl.multiple_of((h // 8) * 8, 8), 8)
    rows = ref[0, tile, lanes] if batched else ref[tile, lanes]
    picked = lax.broadcasted_iota(jnp.int32, rows.shape, 0) == h % 8
    return jnp.sum(jnp.where(picked, rows, jnp.zeros_like(rows)), axis=0, keepdims=True)


def lanes_of(h):
    return pl.ds(pl.multiple_of(h * HEAD_DIM, HEAD_DIM), HEAD_DIM)


def sum_head(h, starts_ref, codes_ref, keys, values, kin, vin, early_sums, firsts):
    f0 = starts_ref[0, 0].astype(F32)
    f1 = starts_ref[0, 1].astype(F32)
    s1 = 1.0 - f1
    code_iota = lax.broadcasted_iota(jnp.int32, (CODES, BLOCK), 0)
    lane = lax.broadcasted_iota(jnp.int32, (BLOCK, 128), 1).astype(F32)
    place = lax.broadcasted_iota(jnp.int32, (BLOCK, 128), 0).astype(F32)
    sums, counts = [], []
    for b in range(2):
        rows = slice(b * BLOCK, (b + 1) * BLOCK)
        code_row = head_row(codes_ref, h, rows, True)
        hot = jnp.where(code_iota == code_row, 1.0, 0.0).astype(BF16)
        pair = jnp.concatenate([keys[rows, lanes_of(h)], values[rows, lanes_of(h)]], axis=1)
        sums.append(jnp.dot(hot, pair, preferred_element_type=F32))
        code_col = jnp.broadcast_to(code_row.astype(F32), (128, BLOCK)).T
        counted = []
        for r in range(4):
            same = code_col == lane + 128.0 * r
            counted.append(jnp.sum(jnp.where(same, 1.0, 0.0), axis=0, keepdims=True))
            firsts[h, b : b + 1, r * 128 : (r + 1) * 128] = jnp.min(
                jnp.where(same, place, float(BLOCK)), axis=0, keepdims=True
            )
        counts.append(counted)
    flag = jnp.broadcast_to(jnp.maximum(f0, f1), (1, 128))
    none = jnp.zeros((1, 128), F32)
    pad = jnp.zeros((5, 128), F32)
    for g in range(2):
        part = slice(g * 256, (g + 1) * 256)
        at = 2 * h + g
        first = [counts[0][2 * g], counts[0][2 * g + 1]]
        second = [counts[1][2 * g], counts[1][2 * g + 1]]
        both = [first[i] + second[i] for i in range(2)]
        tail = [s1 * first[i] + second[i] for i in range(2)]
        kin[at, 0:256, :] = sums[0][part, :128] + sums[1][part, :128]
        kin[at, 256:264, :] = jnp.concatenate(both + [none, pad], axis=0)
        vin[at, 0:256, :] = s1 * sums[0][part, 128:] + sums[1][part, 128:]
        vin[at, 256:264, :] = jnp.concatenate(tail + [flag, pad], axis=0)
        early_sums[at, 0:256, :] = sums[0][part, 128:]
        early_sums[at, 256:264, :] = jnp.concatenate(first + [flag, pad], axis=0)


def unpacked(ref, h):
    a, b = 2 * h, 2 * h + 1
    sums = jnp.concatenate([ref[a, 0:256, :], ref[b, 0:256, :]], axis=0)
    low, high = ref[a, 256:264, :], ref[b, 256:264, :]
    return sums, [low[0:1], low[1:2], high[0:1], high[1:2]]


def attend_head(
    h, dp, starts_ref, codes_ref, old_ref, queries, values, kout, vout, early_sums, firsts,
    centroids, book_ref, out_ref, share_ref,
):
    alive = [1.0 - starts_ref[0, b].astype(F32) for b in range(2)]
    key_sums, key_counts = unpacked(kout, h)
    for r in range(4):
        rows = slice(r * 128, (r + 1) * 128)
        old = column(head_row(old_ref, h, rows, False))
        now = column(key_counts[r])
        book_ref[rows, :] = (
            RETAIN * old * centroids[rows, :] + (1.0 - RETAIN) * key_sums[rows]
        ) / (RETAIN * old + (1.0 - RETAIN) * now)
    share_ref[...] = book_ref[pl.ds(pl.multiple_of(dp * 128, 128), 128), :]
    book = book_ref[...].astype(BF16)

    sums, counts = unpacked(vout, h)
    counts = jnp.concatenate(counts, axis=1)
    code_iota = lax.broadcasted_iota(jnp.int32, (CODES, BLOCK), 0)
    square_row = lax.broadcasted_iota(jnp.int32, (128, 128), 0)
    ones_column = jnp.where(
        lax.broadcasted_iota(jnp.int32, (BLOCK, 128), 1) == 0, 1.0, 0.0
    ).astype(BF16)
    half = BLOCK // 2
    causal = lax.broadcasted_iota(jnp.int32, (BLOCK, half), 0) >= lax.broadcasted_iota(
        jnp.int32, (BLOCK, half), 1
    )
    place = lax.broadcasted_iota(jnp.int32, (BLOCK, CODES), 0).astype(F32)
    scores_all = lax.dot_general(
        queries[:, lanes_of(h)], book, (((1,), (1,)), ((), ())), preferred_element_type=F32
    )
    for b in range(2):
        if b == 1:
            more, added = unpacked(early_sums, h)
            sums, counts = sums + more, counts + jnp.concatenate(added, axis=1)
        sums, counts = alive[b] * sums, alive[b] * counts
        present = counts > 0
        bias = jnp.where(present, jnp.log2(jnp.maximum(counts, 1.0)), 0.0)
        opens = jnp.where(present, -1.0, firsts[h, b : b + 1, :])
        high = jnp.floor(counts * (1.0 / 256.0)) * 256.0
        low = counts - high
        columns = []
        for r in range(4):
            lanes = slice(r * 128, (r + 1) * 128)
            columns.append(
                jnp.where(
                    square_row == 0, high[:, lanes], jnp.where(square_row == 1, low[:, lanes], 0.0)
                ).T
            )
        cache = jnp.concatenate([sums, jnp.concatenate(columns, axis=0)], axis=1).astype(BF16)
        rows = slice(b * BLOCK, (b + 1) * BLOCK)
        code_row = head_row(codes_ref, h, rows, True)
        hot = jnp.where(code_iota == code_row, 1.0, 0.0).astype(BF16)
        local = jnp.concatenate([values[rows, lanes_of(h)], ones_column], axis=1)
        scores = scores_all[rows] * SCORE_TO_LOG2
        top = jnp.max(jnp.where(opens <= place, scores + bias, NEGATIVE), axis=1, keepdims=True)
        weight = jnp.exp2(jnp.minimum(scores - top, 0.0)).astype(BF16)
        near = jnp.dot(weight, hot[:, :half], preferred_element_type=F32)
        near = jnp.where(causal, near, 0.0).astype(BF16)
        far = jnp.dot(weight[half:], hot[:, half:], preferred_element_type=F32)
        far = jnp.where(causal[:half], far, 0.0).astype(BF16)
        acc = jnp.dot(weight, cache, preferred_element_type=F32)
        acc = acc + jnp.dot(near, local[:half], preferred_element_type=F32)
        acc_far = acc[half:] + jnp.dot(far, local[half:], preferred_element_type=F32)
        acc = acc[:half]
        top_rows = slice(b * BLOCK, b * BLOCK + half)
        low_rows = slice(b * BLOCK + half, (b + 1) * BLOCK)
        out_ref[top_rows, :] = (acc[:, :128] / (acc[:, 128:129] + acc[:, 129:130])).astype(BF16)
        out_ref[low_rows, :] = (
            acc_far[:, :128] / (acc_far[:, 128:129] + acc_far[:, 129:130])
        ).astype(BF16)


def layer_kernel(
    starts_ref, codes_ref, old_ref, q_hbm, k_hbm, v_hbm, cent_hbm, out_hbm, book_hbm,
    kq, values, cents, book_ref, outs, shares, firsts, kin, vin, early_sums, kout, vout,
    kc, vc, ky, s1, kz, xsrc, kx, own, vchip, vx, vz, v2, back,
    k_sem, v_sem, q_sem, cent_sem, out_sem, share_sem, send, recv,
):
    y = lax.axis_index("dp")
    me = lax.axis_index("seq")
    c = me % 2
    x = (me // 2) % 4
    z = me // 8

    def at(dz=0, dx=0, dc=0):
        return {"seq": (((z + dz) % 4) * 4 + (x + dx) % 4) * 2 + (c + dc) % 2}

    def at_y(dy):
        return {"dp": (y + dy) % 4}

    def remote(src, dst, phase, g, device):
        return pltpu.make_async_remote_copy(
            src_ref=src, dst_ref=dst, send_sem=send.at[phase, g], recv_sem=recv.at[phase, g],
            device_id=device, device_id_type=MESH,
        )

    def four(g):
        return vchip.at[g]

    def three(g):
        return vchip.at[g, pl.ds(0, 3)]

    def three_slices(g):
        return s1.at[g, pl.ds(0, 3)]

    def three_rows(g):
        return vchip.at[g, 0, pl.ds(0, 192)]

    sizes = {
        KEY_CORE: four, VAL_CORE: four, KEY_Y: three, VAL_X: three, KEY_Z: three_slices,
        VAL_Z: three, KEY_X: three_slices, VAL_BACK: three, KEY_ZB: three_rows, KEY_YB: three,
        KEY_CB: four, VAL_CB: four,
    }

    def arrived(phase, g):
        part = sizes[phase](g)
        remote(part, part, phase, g, at(dc=1)).wait_recv()

    def left(phase, g):
        part = sizes[phase](g)
        remote(part, part, phase, g, at(dc=1)).wait_send()

    def unit_loop(body):
        def step(u, carry):
            body(u)
            return carry

        lax.fori_loop(0, 4, step, 0)

    def columns_of(g):
        return pl.ds(pl.multiple_of(g * 512, 512), 512)

    def load_keys(g):
        return pltpu.make_async_copy(k_hbm.at[0, :, columns_of(g)], kq.at[:, columns_of(g)], k_sem.at[g])

    def load_values(g):
        return pltpu.make_async_copy(v_hbm.at[0, :, columns_of(g)], values.at[:, columns_of(g)], v_sem.at[g])

    def load_queries():
        return pltpu.make_async_copy(q_hbm.at[0], kq, q_sem)

    def load_centroids(h):
        return pltpu.make_async_copy(cent_hbm.at[h], cents.at[h % 2], cent_sem.at[h % 2])

    def store_out(h):
        return pltpu.make_async_copy(outs.at[h % 2], out_hbm.at[0, :, lanes_of(h)], out_sem.at[h % 2])

    def store_share(h):
        return pltpu.make_async_copy(shares.at[h % 2], book_hbm.at[h], share_sem.at[h % 2])

    for g in range(GROUPS):
        load_keys(g).start()
        load_values(g).start()
    for h in range(2):
        load_centroids(h).start()

    barrier = pltpu.get_barrier_semaphore()

    def greet(device):
        pl.semaphore_signal(barrier, inc=1, device_id=device, device_id_type=MESH)

    greet(at(dc=1))
    for k in (1, 2, 3):
        greet(at(dx=k))
        greet(at(dz=k))
        greet(at_y(k))
    pl.semaphore_wait(barrier, 10)

    def share_cores(g):
        theirs = pl.ds(8 * g + 4 * (1 - c), 4)
        remote(kin.at[theirs], kc.at[g], KEY_CORE, g, at(dc=1)).start()
        remote(vin.at[theirs], vc.at[g], VAL_CORE, g, at(dc=1)).start()

    def join(g):
        mine = 8 * g + 4 * c
        arrived(KEY_CORE, g)

        def add(u):
            kc[g, u] = kc[g, u] + kin[mine + u]

        unit_loop(add)
        for k in (1, 2, 3):
            remote(kc.at[g, (y + k) % 4], ky.at[g, 3 - k], KEY_Y, g, at_y(k)).start()
        arrived(VAL_CORE, g)

        def link(u):
            ours = vin[mine + u]
            theirs = vc[g, u]
            early = jnp.where(c == 0, ours, theirs)
            late = jnp.where(c == 0, theirs, ours)
            vchip[g, u] = late + (1.0 - late[258:259, :]) * early

        unit_loop(link)
        for k in (1, 2, 3):
            remote(vchip.at[g, (x + k) % 4], vx.at[g, x], VAL_X, g, at(dx=k)).start()
        vx[g, x] = vchip[g, x]

    def keys_y(g):
        arrived(KEY_Y, g)

        def add(i):
            rows = pl.ds(pl.multiple_of(i * 64, 64), 64)
            s1[g, i, 0:64, :] = (kc[g, y, rows, :] + ky[g, 0, rows, :]) + (
                ky[g, 1, rows, :] + ky[g, 2, rows, :]
            )
            s1[g, i, 64:72, :] = (kc[g, y, 256:264, :] + ky[g, 0, 256:264, :]) + (
                ky[g, 1, 256:264, :] + ky[g, 2, 256:264, :]
            )

        unit_loop(add)
        for k in (1, 2, 3):
            remote(s1.at[g, (z + k) % 4], kz.at[g, 3 - k], KEY_Z, g, at(dz=k)).start()

    def keys_z(g):
        arrived(KEY_Z, g)
        part = (s1[g, z] + kz[g, 0]) + (kz[g, 1] + kz[g, 2])
        xsrc[g] = part
        kx[g, x] = part
        for k in (1, 2, 3):
            remote(xsrc.at[g], kx.at[g, x], KEY_X, g, at(dx=k)).start()

    def slice_of_unit():
        return pl.ds(pl.multiple_of(z * 64, 64), 64)

    def keys_x(g):
        arrived(KEY_X, g)
        total = (kx[g, 0] + kx[g, 1]) + (kx[g, 2] + kx[g, 3])
        unit = 8 * g + 4 * c + y
        own[g] = total[0:64]
        kout[unit, slice_of_unit(), :] = total[0:64]
        kout[unit, 256:264, :] = total[64:72]
        for k in (1, 2, 3):
            remote(own.at[g], kout.at[unit, slice_of_unit()], KEY_ZB, g, at(dz=k)).start()

    def keys_back_z(g):
        arrived(KEY_ZB, g)
        unit = kout.at[8 * g + 4 * c + y]
        for k in (1, 2, 3):
            remote(unit, unit, KEY_YB, g, at_y(k)).start()

    def keys_back_y(g):
        arrived(KEY_YB, g)
        mine = kout.at[pl.ds(8 * g + 4 * c, 4)]
        remote(mine, mine, KEY_CB, g, at(dc=1)).start()

    def scan_row(g):
        arrived(VAL_X, g)

        def step(j, run):
            part = vx[g, j]
            vx[g, j] = run
            return part + (1.0 - part[258:259, :]) * run

        vz[g, z] = lax.fori_loop(0, 4, step, jnp.zeros((UNIT, 128), F32))
        for k in (1, 2, 3):
            remote(vz.at[g, z], vz.at[g, z], VAL_Z, g, at(dz=k)).start()

    def scan_rows(g):
        arrived(VAL_Z, g)

        def step(j, run):
            part = vz[g, j]
            return jnp.where(j < z, part + (1.0 - part[258:259, :]) * run, run)

        ahead = lax.fori_loop(0, 3, step, jnp.zeros((UNIT, 128), F32))

        def enter(j):
            part = vx[g, j]
            vx[g, j] = part + (1.0 - part[258:259, :]) * ahead

        unit_loop(enter)
        for k in (1, 2, 3):
            remote(vx.at[g, (x + k) % 4], v2.at[g, x], VAL_BACK, g, at(dx=k)).start()
        v2[g, x] = vx[g, x]

    def split(g):
        arrived(VAL_BACK, g)
        mine = 8 * g + 4 * c

        def part(u):
            early = jnp.where(c == 0, vin[mine + u], vc[g, u])
            first = v2[g, u]
            second = early + (1.0 - early[258:259, :]) * first
            vout[mine + u] = jnp.where(c == 0, first, second)
            back[g, u] = jnp.where(c == 0, second, first)

        unit_loop(part)
        remote(back.at[g], vout.at[pl.ds(mine, 4)], VAL_CB, g, at(dc=1)).start()

    def step(tick, carry):
        @pl.when(tick < HEADS)
        def _():
            h = tick
            g = h // 4

            @pl.when(h % 4 == 0)
            def _():
                load_keys(g).wait()
                load_values(g).wait()

            sum_head(h, starts_ref, codes_ref, kq, values, kin, vin, early_sums, firsts)

            @pl.when(h % 4 == 3)
            def _():
                share_cores(g)

            @pl.when(h == HEADS - 1)
            def _():
                load_queries().start()

        @pl.when(tick >= ATTEND)
        def _():
            h = tick - ATTEND
            g = h // 4

            @pl.when(h == 0)
            def _():
                load_queries().wait()

            @pl.when(h % 4 == 0)
            def _():
                arrived(KEY_CB, g)
                arrived(VAL_CB, g)

            load_centroids(h).wait()

            @pl.when(h >= 2)
            def _():
                store_out(h - 2).wait()
                store_share(h - 2).wait()

            attend_head(
                h, y, starts_ref, codes_ref, old_ref, kq, values, kout, vout, early_sums, firsts,
                cents.at[h % 2], book_ref, outs.at[h % 2], shares.at[h % 2],
            )
            store_out(h).start()
            store_share(h).start()

            @pl.when(h + 2 < HEADS)
            def _():
                load_centroids(h + 2).start()

        for when, stage in (
            (AT_YB, keys_back_y), (AT_SPLIT, split), (AT_ZB, keys_back_z), (AT_X, keys_x),
            (AT_Z, keys_z), (AT_ROWS, scan_rows), (AT_Y, keys_y), (AT_SCAN, scan_row),
            (AT_JOIN, join),
        ):
            first, stride = when
            since = tick - first

            @pl.when((since >= 0) & (since % stride == 0) & (since < GROUPS * stride))
            def _(stage=stage, since=since, stride=stride):
                stage(since // stride)

        return carry

    lax.fori_loop(0, ATTEND + HEADS, step, 0)

    for h in (HEADS - 2, HEADS - 1):
        store_out(h).wait()
        store_share(h).wait()

    def finish(g, carry):
        for phase in range(PHASES):
            left(phase, g)
        return carry

    lax.fori_loop(0, GROUPS, finish, 0)


def layer(queries, keys, values, codes, starts, centroids, old):
    anywhere = pl.BlockSpec(memory_space=pl.ANY)
    whole = pl.BlockSpec(memory_space=pltpu.VMEM)

    def units(*shape):
        return pltpu.VMEM((*shape, 128), F32)

    return pl.pallas_call(
        layer_kernel,
        name="layer",
        out_shape=(
            jax.ShapeDtypeStruct((1, TOK_DEV, HEADS * HEAD_DIM), BF16),
            jax.ShapeDtypeStruct((HEADS, CODES // 4, HEAD_DIM), F32),
        ),
        in_specs=[pl.BlockSpec(memory_space=pltpu.SMEM), whole, whole] + [anywhere] * 4,
        out_specs=[anywhere, anywhere],
        scratch_shapes=[
            pltpu.VMEM((TOK_DEV, HEADS * HEAD_DIM), BF16),
            pltpu.VMEM((TOK_DEV, HEADS * HEAD_DIM), BF16),
            units(2, CODES),
            units(CODES),
            pltpu.VMEM((2, TOK_DEV, HEAD_DIM), BF16),
            units(2, CODES // 4),
            pltpu.VMEM((HEADS, 8, CODES), F32),
            units(32, UNIT),
            units(32, UNIT),
            units(32, UNIT),
            units(32, UNIT),
            units(32, UNIT),
            units(GROUPS, 4, UNIT),
            units(GROUPS, 4, UNIT),
            units(GROUPS, 3, UNIT),
            units(GROUPS, 4, 72),
            units(GROUPS, 3, 72),
            units(GROUPS, 72),
            units(GROUPS, 4, 72),
            units(GROUPS, 64),
            units(GROUPS, 4, UNIT),
            units(GROUPS, 4, UNIT),
            units(GROUPS, 4, UNIT),
            units(GROUPS, 4, UNIT),
            units(GROUPS, 4, UNIT),
            pltpu.SemaphoreType.DMA((GROUPS,)),
            pltpu.SemaphoreType.DMA((GROUPS,)),
            pltpu.SemaphoreType.DMA,
            pltpu.SemaphoreType.DMA((2,)),
            pltpu.SemaphoreType.DMA((2,)),
            pltpu.SemaphoreType.DMA((2,)),
            pltpu.SemaphoreType.DMA((PHASES, GROUPS)),
            pltpu.SemaphoreType.DMA((PHASES, GROUPS)),
        ],
        compiler_params=pltpu.CompilerParams(
            collective_id=0, has_side_effects=True, vmem_limit_bytes=63 << 20
        ),
    )(starts, codes, old, queries, keys, values, centroids)


def shards(queries, keys, values, codes, starts, old_centroids, old_counts):
    return layer(queries, keys, values, codes, starts, old_centroids, old_counts)


def solution(mesh):
    placed = (
        P("dp", "seq", None),
        P("dp", "seq", None),
        P("dp", "seq", None),
        P("dp", None, "seq"),
        P("dp", "seq"),
        P(),
        P(),
    )
    return jax.shard_map(
        shards,
        mesh=mesh,
        in_specs=placed,
        out_specs=(P("dp", "seq", None), P(None, "dp", None)),
        check_vma=False,
    )
```

```python
import jax
import jax.numpy as jnp
from jax import lax
from jax.experimental import pallas as pl
from jax.experimental.pallas import tpu as pltpu
from jax.sharding import PartitionSpec as P

HEADS = 16
HEAD_DIM = 128
CODES = 512
BLOCK = 512
TOK_DEV = 1024
RETAIN = 0.9
NEGATIVE = -1e30
SCORE_TO_LOG2 = 1.4426950408889634 * HEAD_DIM**-0.5

UNIT = 136
UNITS = 64
GROUPS = 8
PER_GROUP = 2
PART = 32
SLICE = PART + 8
F32 = jnp.float32
BF16 = jnp.bfloat16
MESH = pl.DeviceIdType.MESH

(KEY_CORE, VAL_CORE, KEY_Y, VAL_X, KEY_Z, VAL_Z, KEY_X, VAL_BACK, KEY_ZB, KEY_YB, KEY_CB, VAL_CB) = range(12)
PHASES = 12

ATTEND = 16
AT_JOIN = (3, 2)
AT_Y = (6, 2)
AT_SCAN = (7, 2)
AT_Z = (8, 2)
AT_ROWS = (10, 2)
AT_X = (11, 2)
AT_ZB = (12, 2)
AT_SPLIT = (14, 2)
AT_YB = (14, 2)


def column(row):
    return jnp.broadcast_to(row, (128, 128)).T


def head_row(ref, h, lanes, batched):
    tile = pl.ds(pl.multiple_of((h // 8) * 8, 8), 8)
    rows = ref[0, tile, lanes] if batched else ref[tile, lanes]
    picked = lax.broadcasted_iota(jnp.int32, rows.shape, 0) == h % 8
    return jnp.sum(jnp.where(picked, rows, jnp.zeros_like(rows)), axis=0, keepdims=True)


def lanes_of(h):
    return pl.ds(pl.multiple_of(h * HEAD_DIM, HEAD_DIM), HEAD_DIM)


def sum_head(h, starts_ref, codes_ref, keys, values, kin, vin, early_sums, firsts):
    f0 = starts_ref[0, 0].astype(F32)
    f1 = starts_ref[0, 1].astype(F32)
    s1 = 1.0 - f1
    code_iota = lax.broadcasted_iota(jnp.int32, (CODES, BLOCK), 0)
    lane = lax.broadcasted_iota(jnp.int32, (BLOCK, 128), 1).astype(F32)
    place = lax.broadcasted_iota(jnp.int32, (BLOCK, 128), 0).astype(F32)
    sums, counts = [], []
    for b in range(2):
        rows = slice(b * BLOCK, (b + 1) * BLOCK)
        code_row = head_row(codes_ref, h, rows, True)
        hot = jnp.where(code_iota == code_row, 1.0, 0.0).astype(BF16)
        pair = jnp.concatenate([keys[rows, lanes_of(h)], values[rows, lanes_of(h)]], axis=1)
        sums.append(jnp.dot(hot, pair, preferred_element_type=F32))
        code_col = jnp.broadcast_to(code_row.astype(F32), (128, BLOCK)).T
        counted = []
        for r in range(4):
            same = code_col == lane + 128.0 * r
            counted.append(jnp.sum(jnp.where(same, 1.0, 0.0), axis=0, keepdims=True))
            firsts[h, b : b + 1, r * 128 : (r + 1) * 128] = jnp.min(
                jnp.where(same, place, float(BLOCK)), axis=0, keepdims=True
            )
        counts.append(counted)
    flag = jnp.broadcast_to(jnp.maximum(f0, f1), (1, 128))
    none = jnp.zeros((1, 128), F32)
    pad = jnp.zeros((6, 128), F32)
    for i in range(4):
        part = slice(i * 128, (i + 1) * 128)
        at = 4 * h + i
        first, second = counts[0][i], counts[1][i]
        kin[at, 0:128, :] = sums[0][part, :128] + sums[1][part, :128]
        kin[at, 128:136, :] = jnp.concatenate([first + second, none, pad], axis=0)
        vin[at, 0:128, :] = s1 * sums[0][part, 128:] + sums[1][part, 128:]
        vin[at, 128:136, :] = jnp.concatenate([s1 * first + second, flag, pad], axis=0)
        early_sums[at, 0:128, :] = sums[0][part, 128:]
        early_sums[at, 128:136, :] = jnp.concatenate([first, flag, pad], axis=0)


def unpacked(ref, h):
    sums = jnp.concatenate([ref[4 * h + i, 0:128, :] for i in range(4)], axis=0)
    return sums, [ref[4 * h + i, 128:136, :][0:1] for i in range(4)]


def attend_head(
    h, dp, starts_ref, codes_ref, old_ref, queries, values, kout, vout, early_sums, firsts,
    centroids, book_ref, out_ref, share_ref,
):
    alive = [1.0 - starts_ref[0, b].astype(F32) for b in range(2)]
    key_sums, key_counts = unpacked(kout, h)
    for r in range(4):
        rows = slice(r * 128, (r + 1) * 128)
        old = column(head_row(old_ref, h, rows, False))
        now = column(key_counts[r])
        book_ref[rows, :] = (
            RETAIN * old * centroids[rows, :] + (1.0 - RETAIN) * key_sums[rows]
        ) / (RETAIN * old + (1.0 - RETAIN) * now)
    share_ref[...] = book_ref[pl.ds(pl.multiple_of(dp * 128, 128), 128), :]
    book = book_ref[...].astype(BF16)

    sums, counts = unpacked(vout, h)
    counts = jnp.concatenate(counts, axis=1)
    code_iota = lax.broadcasted_iota(jnp.int32, (CODES, BLOCK), 0)
    square_row = lax.broadcasted_iota(jnp.int32, (128, 128), 0)
    ones_column = jnp.where(
        lax.broadcasted_iota(jnp.int32, (BLOCK, 128), 1) == 0, 1.0, 0.0
    ).astype(BF16)
    half = BLOCK // 2
    causal = lax.broadcasted_iota(jnp.int32, (BLOCK, half), 0) >= lax.broadcasted_iota(
        jnp.int32, (BLOCK, half), 1
    )
    place = lax.broadcasted_iota(jnp.int32, (BLOCK, CODES), 0).astype(F32)
    scores_all = lax.dot_general(
        queries[:, lanes_of(h)], book, (((1,), (1,)), ((), ())), preferred_element_type=F32
    )
    for b in range(2):
        if b == 1:
            more, added = unpacked(early_sums, h)
            sums, counts = sums + more, counts + jnp.concatenate(added, axis=1)
        sums, counts = alive[b] * sums, alive[b] * counts
        present = counts > 0
        bias = jnp.where(present, jnp.log2(jnp.maximum(counts, 1.0)), 0.0)
        opens = jnp.where(present, -1.0, firsts[h, b : b + 1, :])
        high = jnp.floor(counts * (1.0 / 256.0)) * 256.0
        low = counts - high
        columns = []
        for r in range(4):
            lanes = slice(r * 128, (r + 1) * 128)
            columns.append(
                jnp.where(
                    square_row == 0, high[:, lanes], jnp.where(square_row == 1, low[:, lanes], 0.0)
                ).T
            )
        cache = jnp.concatenate([sums, jnp.concatenate(columns, axis=0)], axis=1).astype(BF16)
        rows = slice(b * BLOCK, (b + 1) * BLOCK)
        code_row = head_row(codes_ref, h, rows, True)
        hot = jnp.where(code_iota == code_row, 1.0, 0.0).astype(BF16)
        local = jnp.concatenate([values[rows, lanes_of(h)], ones_column], axis=1)
        scores = scores_all[rows] * SCORE_TO_LOG2
        top = jnp.max(jnp.where(opens <= place, scores + bias, NEGATIVE), axis=1, keepdims=True)
        weight = jnp.exp2(jnp.minimum(scores - top, 0.0)).astype(BF16)
        near = jnp.dot(weight, hot[:, :half], preferred_element_type=F32)
        near = jnp.where(causal, near, 0.0).astype(BF16)
        far = jnp.dot(weight[half:], hot[:, half:], preferred_element_type=F32)
        far = jnp.where(causal[:half], far, 0.0).astype(BF16)
        acc = jnp.dot(weight, cache, preferred_element_type=F32)
        acc = acc + jnp.dot(near, local[:half], preferred_element_type=F32)
        acc_far = acc[half:] + jnp.dot(far, local[half:], preferred_element_type=F32)
        acc = acc[:half]
        top_rows = slice(b * BLOCK, b * BLOCK + half)
        low_rows = slice(b * BLOCK + half, (b + 1) * BLOCK)
        out_ref[top_rows, :] = (acc[:, :128] / (acc[:, 128:129] + acc[:, 129:130])).astype(BF16)
        out_ref[low_rows, :] = (
            acc_far[:, :128] / (acc_far[:, 128:129] + acc_far[:, 129:130])
        ).astype(BF16)


def layer_kernel(
    starts_ref, codes_ref, old_ref, q_hbm, k_hbm, v_hbm, cent_hbm, out_hbm, book_hbm,
    kq, values, cents, book_ref, outs, shares, firsts, kin, vin, early_sums, kout, vout,
    kc, vc, ky, s1, kz, xsrc, kx, own, vchip, vx, vz, v2, back,
    k_sem, v_sem, q_sem, cent_sem, out_sem, share_sem, send, recv,
):
    y = lax.axis_index("dp")
    me = lax.axis_index("seq")
    c = me % 2
    x = (me // 2) % 4
    z = me // 8

    def at(dz=0, dx=0, dc=0):
        return {"seq": (((z + dz) % 4) * 4 + (x + dx) % 4) * 2 + (c + dc) % 2}

    def at_y(dy):
        return {"dp": (y + dy) % 4}

    def remote(src, dst, phase, g, device):
        return pltpu.make_async_remote_copy(
            src_ref=src, dst_ref=dst, send_sem=send.at[phase, g], recv_sem=recv.at[phase, g],
            device_id=device, device_id_type=MESH,
        )

    def four(g):
        return vchip.at[g]

    def three(g):
        return vchip.at[g, pl.ds(0, 3)]

    def three_slices(g):
        return s1.at[g, pl.ds(0, 3)]

    def three_rows(g):
        return vchip.at[g, 0, pl.ds(0, 3 * PART)]

    sizes = {
        KEY_CORE: four, VAL_CORE: four, KEY_Y: three, VAL_X: three, KEY_Z: three_slices,
        VAL_Z: three, KEY_X: three_slices, VAL_BACK: three, KEY_ZB: three_rows, KEY_YB: three,
        KEY_CB: four, VAL_CB: four,
    }

    def arrived(phase, g):
        part = sizes[phase](g)
        remote(part, part, phase, g, at(dc=1)).wait_recv()

    def left(phase, g):
        part = sizes[phase](g)
        remote(part, part, phase, g, at(dc=1)).wait_send()

    def unit_loop(body):
        def step(u, carry):
            body(u)
            return carry

        lax.fori_loop(0, 4, step, 0)

    def columns_of(g):
        return pl.ds(pl.multiple_of(g * 256, 256), 256)

    def load_keys(g):
        return pltpu.make_async_copy(k_hbm.at[0, :, columns_of(g)], kq.at[:, columns_of(g)], k_sem.at[g])

    def load_values(g):
        return pltpu.make_async_copy(v_hbm.at[0, :, columns_of(g)], values.at[:, columns_of(g)], v_sem.at[g])

    def load_queries():
        return pltpu.make_async_copy(q_hbm.at[0], kq, q_sem)

    def load_centroids(h):
        return pltpu.make_async_copy(cent_hbm.at[h], cents.at[h % 2], cent_sem.at[h % 2])

    def store_out(h):
        return pltpu.make_async_copy(outs.at[h % 2], out_hbm.at[0, :, lanes_of(h)], out_sem.at[h % 2])

    def store_share(h):
        return pltpu.make_async_copy(shares.at[h % 2], book_hbm.at[h], share_sem.at[h % 2])

    for g in range(GROUPS):
        load_keys(g).start()
        load_values(g).start()
    for h in range(2):
        load_centroids(h).start()

    barrier = pltpu.get_barrier_semaphore()

    def greet(device):
        pl.semaphore_signal(barrier, inc=1, device_id=device, device_id_type=MESH)

    greet(at(dc=1))
    for k in (1, 2, 3):
        greet(at(dx=k))
        greet(at(dz=k))
        greet(at_y(k))
    pl.semaphore_wait(barrier, 10)

    def share_cores(g):
        theirs = pl.ds(8 * g + 4 * (1 - c), 4)
        remote(kin.at[theirs], kc.at[g], KEY_CORE, g, at(dc=1)).start()
        remote(vin.at[theirs], vc.at[g], VAL_CORE, g, at(dc=1)).start()

    def join(g):
        mine = 8 * g + 4 * c
        arrived(KEY_CORE, g)

        def add(u):
            kc[g, u] = kc[g, u] + kin[mine + u]

        unit_loop(add)
        for k in (1, 2, 3):
            remote(kc.at[g, (y + k) % 4], ky.at[g, 3 - k], KEY_Y, g, at_y(k)).start()
        arrived(VAL_CORE, g)

        def link(u):
            ours = vin[mine + u]
            theirs = vc[g, u]
            early = jnp.where(c == 0, ours, theirs)
            late = jnp.where(c == 0, theirs, ours)
            vchip[g, u] = late + (1.0 - late[129:130, :]) * early

        unit_loop(link)
        for k in (1, 2, 3):
            remote(vchip.at[g, (x + k) % 4], vx.at[g, x], VAL_X, g, at(dx=k)).start()
        vx[g, x] = vchip[g, x]

    def keys_y(g):
        arrived(KEY_Y, g)

        def add(i):
            rows = pl.ds(pl.multiple_of(i * PART, PART), PART)
            s1[g, i, 0:PART, :] = (kc[g, y, rows, :] + ky[g, 0, rows, :]) + (
                ky[g, 1, rows, :] + ky[g, 2, rows, :]
            )
            s1[g, i, PART:SLICE, :] = (kc[g, y, 128:136, :] + ky[g, 0, 128:136, :]) + (
                ky[g, 1, 128:136, :] + ky[g, 2, 128:136, :]
            )

        unit_loop(add)
        for k in (1, 2, 3):
            remote(s1.at[g, (z + k) % 4], kz.at[g, 3 - k], KEY_Z, g, at(dz=k)).start()

    def keys_z(g):
        arrived(KEY_Z, g)
        part = (s1[g, z] + kz[g, 0]) + (kz[g, 1] + kz[g, 2])
        xsrc[g] = part
        kx[g, x] = part
        for k in (1, 2, 3):
            remote(xsrc.at[g], kx.at[g, x], KEY_X, g, at(dx=k)).start()

    def slice_of_unit():
        return pl.ds(pl.multiple_of(z * PART, PART), PART)

    def keys_x(g):
        arrived(KEY_X, g)
        total = (kx[g, 0] + kx[g, 1]) + (kx[g, 2] + kx[g, 3])
        unit = 8 * g + 4 * c + y
        own[g] = total[0:PART]
        kout[unit, slice_of_unit(), :] = total[0:PART]
        kout[unit, 128:136, :] = total[PART:SLICE]
        for k in (1, 2, 3):
            remote(own.at[g], kout.at[unit, slice_of_unit()], KEY_ZB, g, at(dz=k)).start()

    def keys_back_z(g):
        arrived(KEY_ZB, g)
        unit = kout.at[8 * g + 4 * c + y]
        for k in (1, 2, 3):
            remote(unit, unit, KEY_YB, g, at_y(k)).start()

    def keys_back_y(g):
        arrived(KEY_YB, g)
        mine = kout.at[pl.ds(8 * g + 4 * c, 4)]
        remote(mine, mine, KEY_CB, g, at(dc=1)).start()

    def scan_row(g):
        arrived(VAL_X, g)

        def step(j, run):
            part = vx[g, j]
            vx[g, j] = run
            return part + (1.0 - part[129:130, :]) * run

        vz[g, z] = lax.fori_loop(0, 4, step, jnp.zeros((UNIT, 128), F32))
        for k in (1, 2, 3):
            remote(vz.at[g, z], vz.at[g, z], VAL_Z, g, at(dz=k)).start()

    def scan_rows(g):
        arrived(VAL_Z, g)

        def step(j, run):
            part = vz[g, j]
            return jnp.where(j < z, part + (1.0 - part[129:130, :]) * run, run)

        ahead = lax.fori_loop(0, 3, step, jnp.zeros((UNIT, 128), F32))

        def enter(j):
            part = vx[g, j]
            vx[g, j] = part + (1.0 - part[129:130, :]) * ahead

        unit_loop(enter)
        for k in (1, 2, 3):
            remote(vx.at[g, (x + k) % 4], v2.at[g, x], VAL_BACK, g, at(dx=k)).start()
        v2[g, x] = vx[g, x]

    def split(g):
        arrived(VAL_BACK, g)
        mine = 8 * g + 4 * c

        def part(u):
            early = jnp.where(c == 0, vin[mine + u], vc[g, u])
            first = v2[g, u]
            second = early + (1.0 - early[129:130, :]) * first
            vout[mine + u] = jnp.where(c == 0, first, second)
            back[g, u] = jnp.where(c == 0, second, first)

        unit_loop(part)
        remote(back.at[g], vout.at[pl.ds(mine, 4)], VAL_CB, g, at(dc=1)).start()

    def step(tick, carry):
        @pl.when(tick < HEADS)
        def _():
            h = tick
            g = h // PER_GROUP

            @pl.when(h % PER_GROUP == 0)
            def _():
                load_keys(g).wait()
                load_values(g).wait()

            sum_head(h, starts_ref, codes_ref, kq, values, kin, vin, early_sums, firsts)

            @pl.when(h % PER_GROUP == PER_GROUP - 1)
            def _():
                share_cores(g)

            @pl.when(h == HEADS - 1)
            def _():
                load_queries().start()

        @pl.when(tick >= ATTEND)
        def _():
            h = tick - ATTEND
            g = h // PER_GROUP

            @pl.when(h == 0)
            def _():
                load_queries().wait()

            @pl.when(h % PER_GROUP == 0)
            def _():
                arrived(KEY_CB, g)
                arrived(VAL_CB, g)

            load_centroids(h).wait()

            @pl.when(h >= 2)
            def _():
                store_out(h - 2).wait()
                store_share(h - 2).wait()

            attend_head(
                h, y, starts_ref, codes_ref, old_ref, kq, values, kout, vout, early_sums, firsts,
                cents.at[h % 2], book_ref, outs.at[h % 2], shares.at[h % 2],
            )
            store_out(h).start()
            store_share(h).start()

            @pl.when(h + 2 < HEADS)
            def _():
                load_centroids(h + 2).start()

        for when, stage in (
            (AT_YB, keys_back_y), (AT_SPLIT, split), (AT_ZB, keys_back_z), (AT_X, keys_x),
            (AT_Z, keys_z), (AT_ROWS, scan_rows), (AT_Y, keys_y), (AT_SCAN, scan_row),
            (AT_JOIN, join),
        ):
            first, stride = when
            since = tick - first

            @pl.when((since >= 0) & (since % stride == 0) & (since < GROUPS * stride))
            def _(stage=stage, since=since, stride=stride):
                stage(since // stride)

        return carry

    lax.fori_loop(0, ATTEND + HEADS, step, 0)

    for h in (HEADS - 2, HEADS - 1):
        store_out(h).wait()
        store_share(h).wait()

    def finish(g, carry):
        for phase in range(PHASES):
            left(phase, g)
        return carry

    lax.fori_loop(0, GROUPS, finish, 0)


def layer(queries, keys, values, codes, starts, centroids, old):
    anywhere = pl.BlockSpec(memory_space=pl.ANY)
    whole = pl.BlockSpec(memory_space=pltpu.VMEM)

    def units(*shape):
        return pltpu.VMEM((*shape, 128), F32)

    return pl.pallas_call(
        layer_kernel,
        name="layer",
        out_shape=(
            jax.ShapeDtypeStruct((1, TOK_DEV, HEADS * HEAD_DIM), BF16),
            jax.ShapeDtypeStruct((HEADS, CODES // 4, HEAD_DIM), F32),
        ),
        in_specs=[pl.BlockSpec(memory_space=pltpu.SMEM), whole, whole] + [anywhere] * 4,
        out_specs=[anywhere, anywhere],
        scratch_shapes=[
            pltpu.VMEM((TOK_DEV, HEADS * HEAD_DIM), BF16),
            pltpu.VMEM((TOK_DEV, HEADS * HEAD_DIM), BF16),
            units(2, CODES),
            units(CODES),
            pltpu.VMEM((2, TOK_DEV, HEAD_DIM), BF16),
            units(2, CODES // 4),
            pltpu.VMEM((HEADS, 8, CODES), F32),
            units(UNITS, UNIT),
            units(UNITS, UNIT),
            units(UNITS, UNIT),
            units(UNITS, UNIT),
            units(UNITS, UNIT),
            units(GROUPS, 4, UNIT),
            units(GROUPS, 4, UNIT),
            units(GROUPS, 3, UNIT),
            units(GROUPS, 4, SLICE),
            units(GROUPS, 3, SLICE),
            units(GROUPS, SLICE),
            units(GROUPS, 4, SLICE),
            units(GROUPS, PART),
            units(GROUPS, 4, UNIT),
            units(GROUPS, 4, UNIT),
            units(GROUPS, 4, UNIT),
            units(GROUPS, 4, UNIT),
            units(GROUPS, 4, UNIT),
            pltpu.SemaphoreType.DMA((GROUPS,)),
            pltpu.SemaphoreType.DMA((GROUPS,)),
            pltpu.SemaphoreType.DMA,
            pltpu.SemaphoreType.DMA((2,)),
            pltpu.SemaphoreType.DMA((2,)),
            pltpu.SemaphoreType.DMA((2,)),
            pltpu.SemaphoreType.DMA((PHASES, GROUPS)),
            pltpu.SemaphoreType.DMA((PHASES, GROUPS)),
        ],
        compiler_params=pltpu.CompilerParams(
            collective_id=0, has_side_effects=True, vmem_limit_bytes=63 << 20
        ),
    )(starts, codes, old, queries, keys, values, centroids)


def shards(queries, keys, values, codes, starts, old_centroids, old_counts):
    return layer(queries, keys, values, codes, starts, old_centroids, old_counts)


def solution(mesh):
    placed = (
        P("dp", "seq", None),
        P("dp", "seq", None),
        P("dp", "seq", None),
        P("dp", None, "seq"),
        P("dp", "seq"),
        P(),
        P(),
    )
    return jax.shard_map(
        shards,
        mesh=mesh,
        in_specs=placed,
        out_specs=(P("dp", "seq", None), P(None, "dp", None)),
        check_vma=False,
    )
```

```python
import jax
import jax.numpy as jnp
from jax import lax
from jax.experimental import pallas as pl
from jax.experimental.pallas import tpu as pltpu
from jax.sharding import PartitionSpec as P

HEADS = 16
HEAD_DIM = 128
CODES = 512
BLOCK = 512
TOK_DEV = 1024
RETAIN = 0.9
NEGATIVE = -1e30
SCORE_TO_LOG2 = 1.4426950408889634 * HEAD_DIM**-0.5

UNIT = 136
UNITS = 64
GROUPS = 8
PER_GROUP = 2
PART = 32
SLICE = PART + 8
F32 = jnp.float32
BF16 = jnp.bfloat16
MESH = pl.DeviceIdType.MESH

(KEY_CORE, VAL_CORE, KEY_Y, VAL_X, KEY_Z, VAL_Z, KEY_X, VAL_BACK, KEY_ZB, KEY_YB, KEY_CB, VAL_CB) = range(12)
PHASES = 12

ATTEND = 9
AT_JOIN = (1, 2, 3, 4, 5, 6, 7, 8)
AT_Y = (3, 4, 5, 6, 6, 7, 8, 9)
AT_SCAN = (3, 4, 5, 7, 7, 8, 10, 10)
AT_Z = (4, 5, 6, 7, 7, 8, 10, 10)
AT_ROWS = (5, 6, 7, 8, 9, 10, 11, 12)
AT_X = (5, 6, 7, 8, 8, 10, 11, 11)
AT_ZB = (6, 7, 8, 9, 9, 11, 12, 12)
AT_SPLIT = (7, 8, 9, 10, 11, 12, 13, 14)
AT_YB = (7, 8, 9, 10, 11, 12, 13, 14)


def groups_before(when, tick):
    count = 0
    for at in when:
        count = count + jnp.minimum(jnp.maximum(tick - at, 0), 1)
    return count


def column(row):
    return jnp.broadcast_to(row, (128, 128)).T


def head_row(ref, h, lanes, batched):
    tile = pl.ds(pl.multiple_of((h // 8) * 8, 8), 8)
    rows = ref[0, tile, lanes] if batched else ref[tile, lanes]
    picked = lax.broadcasted_iota(jnp.int32, rows.shape, 0) == h % 8
    return jnp.sum(jnp.where(picked, rows, jnp.zeros_like(rows)), axis=0, keepdims=True)


def lanes_of(h):
    return pl.ds(pl.multiple_of(h * HEAD_DIM, HEAD_DIM), HEAD_DIM)


def sum_head(h, starts_ref, codes_ref, keys, values, kin, vin, early_sums, firsts):
    f0 = starts_ref[0, 0].astype(F32)
    f1 = starts_ref[0, 1].astype(F32)
    s1 = 1.0 - f1
    code_iota = lax.broadcasted_iota(jnp.int16, (CODES, BLOCK), 0)
    lane = lax.broadcasted_iota(jnp.int32, (BLOCK, 128), 1).astype(F32)
    place = lax.broadcasted_iota(jnp.int32, (BLOCK, 128), 0).astype(F32)
    sums, counts = [], []
    for b in range(2):
        rows = slice(b * BLOCK, (b + 1) * BLOCK)
        code_row = head_row(codes_ref, h, rows, True)
        hot = jnp.where(code_iota == code_row.astype(jnp.int16), jnp.ones((), BF16), jnp.zeros((), BF16))
        pair = jnp.concatenate([keys[rows, lanes_of(h)], values[rows, lanes_of(h)]], axis=1)
        sums.append(jnp.dot(hot, pair, preferred_element_type=F32))
        code_col = jnp.broadcast_to(code_row.astype(F32), (128, BLOCK)).T
        counted = []
        for r in range(4):
            same = code_col == lane + 128.0 * r
            counted.append(jnp.sum(jnp.where(same, 1.0, 0.0), axis=0, keepdims=True))
            firsts[h, b : b + 1, r * 128 : (r + 1) * 128] = jnp.min(
                jnp.where(same, place, float(BLOCK)), axis=0, keepdims=True
            )
        counts.append(counted)
    flag = jnp.broadcast_to(jnp.maximum(f0, f1), (1, 128))
    none = jnp.zeros((1, 128), F32)
    pad = jnp.zeros((6, 128), F32)
    for i in range(4):
        part = slice(i * 128, (i + 1) * 128)
        at = 4 * h + i
        first, second = counts[0][i], counts[1][i]
        kin[at, 0:128, :] = sums[0][part, :128] + sums[1][part, :128]
        kin[at, 128:136, :] = jnp.concatenate([first + second, none, pad], axis=0)
        vin[at, 0:128, :] = s1 * sums[0][part, 128:] + sums[1][part, 128:]
        vin[at, 128:136, :] = jnp.concatenate([s1 * first + second, flag, pad], axis=0)
        early_sums[at, 0:128, :] = sums[0][part, 128:]
        early_sums[at, 128:136, :] = jnp.concatenate([first, flag, pad], axis=0)


def unpacked(ref, h):
    sums = jnp.concatenate([ref[4 * h + i, 0:128, :] for i in range(4)], axis=0)
    return sums, [ref[4 * h + i, 128:136, :][0:1] for i in range(4)]


def attend_head(
    h, dp, starts_ref, codes_ref, old_ref, queries, values, kout, vout, early_sums, firsts,
    centroids, book_ref, out_ref, share_ref,
):
    alive = [1.0 - starts_ref[0, b].astype(F32) for b in range(2)]
    key_sums, key_counts = unpacked(kout, h)
    for r in range(4):
        rows = slice(r * 128, (r + 1) * 128)
        old = column(head_row(old_ref, h, rows, False))
        now = column(key_counts[r])
        book_ref[rows, :] = (
            RETAIN * old * centroids[rows, :] + (1.0 - RETAIN) * key_sums[rows]
        ) / (RETAIN * old + (1.0 - RETAIN) * now)
    share_ref[...] = book_ref[pl.ds(pl.multiple_of(dp * 128, 128), 128), :]
    book = book_ref[...].astype(BF16)

    sums, counts = unpacked(vout, h)
    counts = jnp.concatenate(counts, axis=1)
    code_iota = lax.broadcasted_iota(jnp.int32, (CODES, BLOCK), 0)
    square_row = lax.broadcasted_iota(jnp.int32, (128, 128), 0)
    ones_column = jnp.where(
        lax.broadcasted_iota(jnp.int32, (BLOCK, 128), 1) == 0, 1.0, 0.0
    ).astype(BF16)
    half = BLOCK // 2
    causal = lax.broadcasted_iota(jnp.int32, (half, half), 0) >= lax.broadcasted_iota(
        jnp.int32, (half, half), 1
    )
    place = lax.broadcasted_iota(jnp.int32, (BLOCK, CODES), 0).astype(F32)
    block_scores = [
        lax.dot_general(
            queries[b * BLOCK : (b + 1) * BLOCK, lanes_of(h)],
            book,
            (((1,), (1,)), ((), ())),
            preferred_element_type=F32,
        )
        for b in range(2)
    ]
    weights, picks, tables = [], [], []
    for b in range(2):
        if b == 1:
            more, added = unpacked(early_sums, h)
            sums, counts = sums + more, counts + jnp.concatenate(added, axis=1)
        sums, counts = alive[b] * sums, alive[b] * counts
        present = counts > 0
        bias = jnp.where(present, jnp.log2(jnp.maximum(counts, 1.0)), 0.0)
        opens = jnp.where(present, -1.0, firsts[h, b : b + 1, :])
        high = jnp.floor(counts * (1.0 / 256.0)) * 256.0
        low = counts - high
        columns = []
        for r in range(4):
            lanes = slice(r * 128, (r + 1) * 128)
            columns.append(
                jnp.where(
                    square_row == 0, high[:, lanes], jnp.where(square_row == 1, low[:, lanes], 0.0)
                ).T
            )
        cache = jnp.concatenate([sums, jnp.concatenate(columns, axis=0)], axis=1).astype(BF16)
        rows = slice(b * BLOCK, (b + 1) * BLOCK)
        code_row = head_row(codes_ref, h, rows, True)
        hot = jnp.where(code_iota == code_row, 1.0, 0.0).astype(BF16)
        local = jnp.concatenate([values[rows, lanes_of(h)], ones_column], axis=1)
        scores = block_scores[b] * SCORE_TO_LOG2
        top = jnp.max(jnp.where(opens <= place, scores + bias, NEGATIVE), axis=1, keepdims=True)
        weights.append(jnp.exp2(jnp.minimum(scores - top, 0.0)).astype(BF16))
        picks.append(hot)
        tables.append(jnp.concatenate([cache, local], axis=0))
    for b in range(2):
        weight, hot, table = weights[b], picks[b], tables[b]
        near = jnp.dot(weight, hot[:, :half], preferred_element_type=F32)
        far = jnp.dot(weight[half:], hot[:, half:], preferred_element_type=F32)
        local_first = jnp.where(causal, near[:half], 0.0).astype(BF16)
        local_second = [near[half:].astype(BF16), jnp.where(causal, far, 0.0).astype(BF16)]
        upper = jnp.concatenate([weight[:half], local_first], axis=1)
        lower = jnp.concatenate([weight[half:]] + local_second, axis=1)
        for i, part in enumerate((upper, lower)):
            acc = jnp.dot(part, table[: part.shape[1]], preferred_element_type=F32)
            rows = slice(b * BLOCK + i * half, b * BLOCK + (i + 1) * half)
            out_ref[rows, :] = (acc[:, :128] / (acc[:, 128:129] + acc[:, 129:130])).astype(BF16)


def layer_kernel(
    starts_ref, codes_ref, old_ref, q_hbm, k_hbm, v_hbm, cent_hbm, out_hbm, book_hbm,
    kq, values, cents, book_ref, outs, shares, firsts, kin, vin, early_sums, kout, vout,
    kc, vc, ky, s1, kz, xsrc, kx, own, vchip, vx, vz, v2, back,
    k_sem, v_sem, q_sem, cent_sem, out_sem, share_sem, send, recv,
):
    y = lax.axis_index("dp")
    me = lax.axis_index("seq")
    c = me % 2
    x = (me // 2) % 4
    z = me // 8

    def at(dz=0, dx=0, dc=0):
        return {"seq": (((z + dz) % 4) * 4 + (x + dx) % 4) * 2 + (c + dc) % 2}

    def at_y(dy):
        return {"dp": (y + dy) % 4}

    def remote(src, dst, phase, g, device):
        return pltpu.make_async_remote_copy(
            src_ref=src, dst_ref=dst, send_sem=send.at[phase, g], recv_sem=recv.at[phase, g],
            device_id=device, device_id_type=MESH,
        )

    def four(g):
        return vchip.at[g]

    def three(g):
        return vchip.at[g, pl.ds(0, 3)]

    def three_slices(g):
        return s1.at[g, pl.ds(0, 3)]

    def three_rows(g):
        return vchip.at[g, 0, pl.ds(0, 3 * PART)]

    sizes = {
        KEY_CORE: four, VAL_CORE: four, KEY_Y: three, VAL_X: three, KEY_Z: three_slices,
        VAL_Z: three, KEY_X: three_slices, VAL_BACK: three, KEY_ZB: three_rows, KEY_YB: three,
        KEY_CB: four, VAL_CB: four,
    }

    def arrived(phase, g):
        part = sizes[phase](g)
        remote(part, part, phase, g, at(dc=1)).wait_recv()

    def left(phase, g):
        part = sizes[phase](g)
        remote(part, part, phase, g, at(dc=1)).wait_send()

    def unit_loop(body):
        def step(u, carry):
            body(u)
            return carry

        lax.fori_loop(0, 4, step, 0)

    def columns_of(g):
        return pl.ds(pl.multiple_of(g * 256, 256), 256)

    def load_keys(g):
        return pltpu.make_async_copy(k_hbm.at[0, :, columns_of(g)], kq.at[:, columns_of(g)], k_sem.at[g])

    def load_values(g):
        return pltpu.make_async_copy(v_hbm.at[0, :, columns_of(g)], values.at[:, columns_of(g)], v_sem.at[g])

    def load_queries():
        return pltpu.make_async_copy(q_hbm.at[0], kq, q_sem)

    def load_centroids(h, slot):
        return pltpu.make_async_copy(cent_hbm.at[h], cents.at[slot], cent_sem.at[slot])

    def store_out(h, slot):
        return pltpu.make_async_copy(outs.at[slot], out_hbm.at[0, :, lanes_of(h)], out_sem.at[slot])

    def store_share(h, slot):
        return pltpu.make_async_copy(shares.at[slot], book_hbm.at[h], share_sem.at[slot])

    for g in range(GROUPS):
        load_keys(g).start()
        load_values(g).start()
    for h in range(2):
        load_centroids(h, h).start()

    def sum_group(g):
        load_keys(g).wait()
        load_values(g).wait()
        for i in range(PER_GROUP):
            sum_head(
                PER_GROUP * g + i, starts_ref, codes_ref, kq, values, kin, vin, early_sums, firsts
            )

    barrier = pltpu.get_barrier_semaphore()

    def greet(device):
        pl.semaphore_signal(barrier, inc=1, device_id=device, device_id_type=MESH)

    greet(at(dc=1))
    for k in (1, 2, 3):
        greet(at(dx=k))
        greet(at(dz=k))
        greet(at_y(k))
    sum_group(0)
    pl.semaphore_wait(barrier, 10)

    def share_cores(g):
        theirs = pl.ds(8 * g + 4 * (1 - c), 4)
        remote(vin.at[theirs], vc.at[g], VAL_CORE, g, at(dc=1)).start()
        remote(kin.at[theirs], kc.at[g], KEY_CORE, g, at(dc=1)).start()

    def join(g):
        mine = 8 * g + 4 * c
        arrived(VAL_CORE, g)

        def link(u):
            ours = vin[mine + u]
            theirs = vc[g, u]
            early = jnp.where(c == 0, ours, theirs)
            late = jnp.where(c == 0, theirs, ours)
            vchip[g, u] = late + (1.0 - late[129:130, :]) * early

        unit_loop(link)
        for k in (1, 2, 3):
            remote(vchip.at[g, (x + k) % 4], vx.at[g, x], VAL_X, g, at(dx=k)).start()
        vx[g, x] = vchip[g, x]
        arrived(KEY_CORE, g)

        def add(u):
            kc[g, u] = kc[g, u] + kin[mine + u]

        unit_loop(add)
        for k in (1, 2, 3):
            remote(kc.at[g, (y + k) % 4], ky.at[g, 3 - k], KEY_Y, g, at_y(k)).start()

    def keys_y(g):
        arrived(KEY_Y, g)

        def add(i):
            rows = pl.ds(pl.multiple_of(i * PART, PART), PART)
            s1[g, i, 0:PART, :] = (kc[g, y, rows, :] + ky[g, 0, rows, :]) + (
                ky[g, 1, rows, :] + ky[g, 2, rows, :]
            )
            s1[g, i, PART:SLICE, :] = (kc[g, y, 128:136, :] + ky[g, 0, 128:136, :]) + (
                ky[g, 1, 128:136, :] + ky[g, 2, 128:136, :]
            )

        unit_loop(add)
        for k in (1, 2, 3):
            remote(s1.at[g, (z + k) % 4], kz.at[g, 3 - k], KEY_Z, g, at(dz=k)).start()

    def keys_z(g):
        arrived(KEY_Z, g)
        part = (s1[g, z] + kz[g, 0]) + (kz[g, 1] + kz[g, 2])
        xsrc[g] = part
        kx[g, x] = part
        for k in (1, 2, 3):
            remote(xsrc.at[g], kx.at[g, x], KEY_X, g, at(dx=k)).start()

    def slice_of_unit():
        return pl.ds(pl.multiple_of(z * PART, PART), PART)

    def keys_x(g):
        arrived(KEY_X, g)
        total = (kx[g, 0] + kx[g, 1]) + (kx[g, 2] + kx[g, 3])
        unit = 8 * g + 4 * c + y
        own[g] = total[0:PART]
        kout[unit, slice_of_unit(), :] = total[0:PART]
        kout[unit, 128:136, :] = total[PART:SLICE]
        for k in (1, 2, 3):
            remote(own.at[g], kout.at[unit, slice_of_unit()], KEY_ZB, g, at(dz=k)).start()

    def keys_back_z(g):
        arrived(KEY_ZB, g)
        unit = kout.at[8 * g + 4 * c + y]
        for k in (1, 2, 3):
            remote(unit, unit, KEY_YB, g, at_y(k)).start()

    def keys_back_y(g):
        arrived(KEY_YB, g)
        mine = kout.at[pl.ds(8 * g + 4 * c, 4)]
        remote(mine, mine, KEY_CB, g, at(dc=1)).start()

    def scan_row(g):
        arrived(VAL_X, g)

        def step(j, run):
            part = vx[g, j]
            vx[g, j] = run
            return part + (1.0 - part[129:130, :]) * run

        vz[g, z] = lax.fori_loop(0, 4, step, jnp.zeros((UNIT, 128), F32))
        for k in (1, 2, 3):
            remote(vz.at[g, z], vz.at[g, z], VAL_Z, g, at(dz=k)).start()

    def scan_rows(g):
        arrived(VAL_Z, g)

        def step(j, run):
            part = vz[g, j]
            return jnp.where(j < z, part + (1.0 - part[129:130, :]) * run, run)

        ahead = lax.fori_loop(0, 3, step, jnp.zeros((UNIT, 128), F32))

        def enter(j):
            part = vx[g, j]
            vx[g, j] = part + (1.0 - part[129:130, :]) * ahead

        unit_loop(enter)
        for k in (1, 2, 3):
            remote(vx.at[g, (x + k) % 4], v2.at[g, x], VAL_BACK, g, at(dx=k)).start()
        v2[g, x] = vx[g, x]

    def split(g):
        arrived(VAL_BACK, g)
        mine = 8 * g + 4 * c

        def part(u):
            early = jnp.where(c == 0, vin[mine + u], vc[g, u])
            first = v2[g, u]
            second = early + (1.0 - early[129:130, :]) * first
            vout[mine + u] = jnp.where(c == 0, first, second)
            back[g, u] = jnp.where(c == 0, second, first)

        unit_loop(part)
        remote(back.at[g], vout.at[pl.ds(mine, 4)], VAL_CB, g, at(dc=1)).start()

    def step(tick, carry):
        @pl.when((tick > 0) & (tick < GROUPS))
        def _():
            g = tick
            sum_group(g)
            share_cores(g)

            @pl.when(g == GROUPS - 1)
            def _():
                load_queries().start()

        @pl.when(tick >= ATTEND)
        def _():
            g = tick - ATTEND

            @pl.when(g == 0)
            def _():
                load_queries().wait()

            @pl.when(g > 0)
            def _():
                for i in range(PER_GROUP):
                    store_out(PER_GROUP * (g - 1) + i, i).wait()
                    store_share(PER_GROUP * (g - 1) + i, i).wait()

            for i in range(PER_GROUP):
                load_centroids(PER_GROUP * g + i, i).wait()
            arrived(KEY_CB, g)
            arrived(VAL_CB, g)
            for i in range(PER_GROUP):
                attend_head(
                    PER_GROUP * g + i, y, starts_ref, codes_ref, old_ref, kq, values, kout, vout,
                    early_sums, firsts, cents.at[i], book_ref.at[i], outs.at[i], shares.at[i],
                )
            for i in range(PER_GROUP):
                store_out(PER_GROUP * g + i, i).start()
                store_share(PER_GROUP * g + i, i).start()

            @pl.when(g + 1 < GROUPS)
            def _():
                for i in range(PER_GROUP):
                    load_centroids(PER_GROUP * (g + 1) + i, i).start()

        for when, stage in (
            (AT_YB, keys_back_y), (AT_SPLIT, split), (AT_ZB, keys_back_z), (AT_X, keys_x),
            (AT_Z, keys_z), (AT_ROWS, scan_rows), (AT_Y, keys_y), (AT_SCAN, scan_row),
            (AT_JOIN, join),
        ):

            def one(g, carry, stage=stage):
                stage(g)
                return carry

            lax.fori_loop(groups_before(when, tick), groups_before(when, tick + 1), one, 0)

        return carry

    share_cores(0)
    lax.fori_loop(1, ATTEND + GROUPS, step, 0)

    for i in range(PER_GROUP):
        store_out(HEADS - PER_GROUP + i, i).wait()
        store_share(HEADS - PER_GROUP + i, i).wait()

    def finish(g, carry):
        for phase in range(PHASES):
            left(phase, g)
        return carry

    lax.fori_loop(0, GROUPS, finish, 0)


def layer(queries, keys, values, codes, starts, centroids, old):
    anywhere = pl.BlockSpec(memory_space=pl.ANY)
    whole = pl.BlockSpec(memory_space=pltpu.VMEM)

    def units(*shape):
        return pltpu.VMEM((*shape, 128), F32)

    return pl.pallas_call(
        layer_kernel,
        name="layer",
        out_shape=(
            jax.ShapeDtypeStruct((1, TOK_DEV, HEADS * HEAD_DIM), BF16),
            jax.ShapeDtypeStruct((HEADS, CODES // 4, HEAD_DIM), F32),
        ),
        in_specs=[pl.BlockSpec(memory_space=pltpu.SMEM), whole, whole] + [anywhere] * 4,
        out_specs=[anywhere, anywhere],
        scratch_shapes=[
            pltpu.VMEM((TOK_DEV, HEADS * HEAD_DIM), BF16),
            pltpu.VMEM((TOK_DEV, HEADS * HEAD_DIM), BF16),
            units(2, CODES),
            units(2, CODES),
            pltpu.VMEM((2, TOK_DEV, HEAD_DIM), BF16),
            units(2, CODES // 4),
            pltpu.VMEM((HEADS, 8, CODES), F32),
            units(UNITS, UNIT),
            units(UNITS, UNIT),
            units(UNITS, UNIT),
            units(UNITS, UNIT),
            units(UNITS, UNIT),
            units(GROUPS, 4, UNIT),
            units(GROUPS, 4, UNIT),
            units(GROUPS, 3, UNIT),
            units(GROUPS, 4, SLICE),
            units(GROUPS, 3, SLICE),
            units(GROUPS, SLICE),
            units(GROUPS, 4, SLICE),
            units(GROUPS, PART),
            units(GROUPS, 4, UNIT),
            units(GROUPS, 4, UNIT),
            units(GROUPS, 4, UNIT),
            units(GROUPS, 4, UNIT),
            units(GROUPS, 4, UNIT),
            pltpu.SemaphoreType.DMA((GROUPS,)),
            pltpu.SemaphoreType.DMA((GROUPS,)),
            pltpu.SemaphoreType.DMA,
            pltpu.SemaphoreType.DMA((2,)),
            pltpu.SemaphoreType.DMA((2,)),
            pltpu.SemaphoreType.DMA((2,)),
            pltpu.SemaphoreType.DMA((PHASES, GROUPS)),
            pltpu.SemaphoreType.DMA((PHASES, GROUPS)),
        ],
        compiler_params=pltpu.CompilerParams(
            collective_id=0, has_side_effects=True, vmem_limit_bytes=63 << 20
        ),
    )(starts, codes, old, queries, keys, values, centroids)


def deliver_kernel(out_hbm, book_hbm, out_to, book_to, rows_held, book_held, sems):
    pieces = []
    for i in range(8):
        rows = pl.ds(i * 128, 128)
        pieces.append((out_hbm.at[0, rows], rows_held.at[rows], out_to.at[0, rows]))
    pieces.append((book_hbm, book_held, book_to))
    inward = [pltpu.make_async_copy(a, b, sems.at[0, i]) for i, (a, b, c) in enumerate(pieces)]
    outward = [pltpu.make_async_copy(b, c, sems.at[1, i]) for i, (a, b, c) in enumerate(pieces)]
    for copy in inward:
        copy.start()
    for arriving, leaving in zip(inward, outward):
        arriving.wait()
        leaving.start()
    for copy in outward:
        copy.wait()


def deliver(out, book):
    hbm = pl.BlockSpec(memory_space=pltpu.HBM)
    return pl.pallas_call(
        deliver_kernel,
        name="deliver",
        out_shape=(
            jax.ShapeDtypeStruct(out.shape, out.dtype),
            jax.ShapeDtypeStruct(book.shape, book.dtype),
        ),
        in_specs=[hbm, hbm],
        out_specs=[hbm, hbm],
        scratch_shapes=[
            pltpu.VMEM(out.shape[1:], out.dtype),
            pltpu.VMEM(book.shape, book.dtype),
            pltpu.SemaphoreType.DMA((2, 9)),
        ],
        compiler_params=pltpu.CompilerParams(vmem_limit_bytes=60 << 20),
    )(out, book)


def shards(queries, keys, values, codes, starts, old_centroids, old_counts):
    return deliver(*layer(queries, keys, values, codes, starts, old_centroids, old_counts))


def solution(mesh):
    placed = (
        P("dp", "seq", None),
        P("dp", "seq", None),
        P("dp", "seq", None),
        P("dp", None, "seq"),
        P("dp", "seq"),
        P(),
        P(),
    )
    return jax.shard_map(
        shards,
        mesh=mesh,
        in_specs=placed,
        out_specs=(P("dp", "seq", None), P(None, "dp", None)),
        check_vma=False,
    )
```

```python
import jax
import jax.numpy as jnp
from jax import lax
from jax.experimental import pallas as pl
from jax.experimental.pallas import tpu as pltpu
from jax.sharding import PartitionSpec as P

HEADS = 16
HEAD_DIM = 128
CODES = 512
BLOCK = 512
TOK_DEV = 1024
RETAIN = 0.9
NEGATIVE = -1e30
SCORE_TO_LOG2 = 1.4426950408889634 * HEAD_DIM**-0.5

UNIT = 136
UNITS = 64
GROUPS = 8
PER_GROUP = 2
PART = 32
SLICE = PART + 8
F32 = jnp.float32
BF16 = jnp.bfloat16
MESH = pl.DeviceIdType.MESH

(KEY_CORE, VAL_CORE, KEY_Y, VAL_X, KEY_Z, VAL_Z, KEY_X, VAL_BACK, KEY_ZB, KEY_YB, KEY_CB, VAL_CB) = range(12)
PHASES = 12

ATTEND = 9
AT_JOIN = (1, 2, 3, 4, 5, 6, 7, 8)
AT_Y = (3, 4, 5, 6, 6, 7, 8, 9)
AT_SCAN = (3, 4, 5, 6, 7, 8, 9, 10)
AT_Z = (4, 5, 6, 7, 7, 8, 10, 10)
AT_ROWS = (5, 6, 7, 8, 9, 10, 11, 11)
AT_X = (5, 6, 7, 8, 8, 10, 11, 11)
AT_ZB = (6, 7, 8, 9, 9, 11, 12, 12)
AT_SPLIT = (7, 8, 9, 10, 11, 12, 12, 13)
AT_YB = (7, 8, 9, 10, 11, 12, 13, 13)


def groups_before(when, tick):
    count = 0
    for at in when:
        count = count + jnp.minimum(jnp.maximum(tick - at, 0), 1)
    return count


def column(row):
    return jnp.broadcast_to(row, (128, 128)).T


def head_row(ref, h, lanes, batched):
    tile = pl.ds(pl.multiple_of((h // 8) * 8, 8), 8)
    rows = ref[0, tile, lanes] if batched else ref[tile, lanes]
    picked = lax.broadcasted_iota(jnp.int32, rows.shape, 0) == h % 8
    return jnp.sum(jnp.where(picked, rows, jnp.zeros_like(rows)), axis=0, keepdims=True)


def lanes_of(h):
    return pl.ds(pl.multiple_of(h * HEAD_DIM, HEAD_DIM), HEAD_DIM)


def sum_head(h, starts_ref, codes_ref, keys, values, kin, vin, early_sums, firsts):
    f0 = starts_ref[0, 0].astype(F32)
    f1 = starts_ref[0, 1].astype(F32)
    s1 = 1.0 - f1
    code_iota = lax.broadcasted_iota(jnp.int16, (CODES, BLOCK), 0)
    lane = lax.broadcasted_iota(jnp.int32, (BLOCK, 128), 1).astype(F32)
    place = lax.broadcasted_iota(jnp.int32, (BLOCK, 128), 0).astype(F32)
    sums, counts = [], []
    for b in range(2):
        rows = slice(b * BLOCK, (b + 1) * BLOCK)
        code_row = head_row(codes_ref, h, rows, True)
        hot = jnp.where(code_iota == code_row.astype(jnp.int16), jnp.ones((), BF16), jnp.zeros((), BF16))
        pair = jnp.concatenate([keys[rows, lanes_of(h)], values[rows, lanes_of(h)]], axis=1)
        sums.append(jnp.dot(hot, pair, preferred_element_type=F32))
        code_col = jnp.broadcast_to(code_row.astype(F32), (128, BLOCK)).T
        counted = []
        for r in range(4):
            same = code_col == lane + 128.0 * r
            counted.append(jnp.sum(jnp.where(same, 1.0, 0.0), axis=0, keepdims=True))
            firsts[h, b : b + 1, r * 128 : (r + 1) * 128] = jnp.min(
                jnp.where(same, place, float(BLOCK)), axis=0, keepdims=True
            )
        counts.append(counted)
    flag = jnp.broadcast_to(jnp.maximum(f0, f1), (1, 128))
    none = jnp.zeros((1, 128), F32)
    pad = jnp.zeros((6, 128), F32)
    for i in range(4):
        part = slice(i * 128, (i + 1) * 128)
        at = 4 * h + i
        first, second = counts[0][i], counts[1][i]
        kin[at, 0:128, :] = sums[0][part, :128] + sums[1][part, :128]
        kin[at, 128:136, :] = jnp.concatenate([first + second, none, pad], axis=0)
        vin[at, 0:128, :] = s1 * sums[0][part, 128:] + sums[1][part, 128:]
        vin[at, 128:136, :] = jnp.concatenate([s1 * first + second, flag, pad], axis=0)
        early_sums[at, 0:128, :] = sums[0][part, 128:]
        early_sums[at, 128:136, :] = jnp.concatenate([first, flag, pad], axis=0)


def unpacked(ref, h):
    sums = jnp.concatenate([ref[4 * h + i, 0:128, :] for i in range(4)], axis=0)
    return sums, [ref[4 * h + i, 128:136, :][0:1] for i in range(4)]


def attend_head(
    h, dp, starts_ref, codes_ref, old_ref, queries, values, kout, vout, early_sums, firsts,
    centroids, book_ref, out_ref, share_ref,
):
    alive = [1.0 - starts_ref[0, b].astype(F32) for b in range(2)]
    key_sums, key_counts = unpacked(kout, h)
    for r in range(4):
        rows = slice(r * 128, (r + 1) * 128)
        old = column(head_row(old_ref, h, rows, False))
        now = column(key_counts[r])
        book_ref[rows, :] = (
            RETAIN * old * centroids[rows, :] + (1.0 - RETAIN) * key_sums[rows]
        ) / (RETAIN * old + (1.0 - RETAIN) * now)
    share_ref[...] = book_ref[pl.ds(pl.multiple_of(dp * 128, 128), 128), :]
    book = book_ref[...].astype(BF16)

    sums, counts = unpacked(vout, h)
    counts = jnp.concatenate(counts, axis=1)
    code_iota = lax.broadcasted_iota(jnp.int32, (CODES, BLOCK), 0)
    square_row = lax.broadcasted_iota(jnp.int32, (128, 128), 0)
    ones_column = jnp.where(
        lax.broadcasted_iota(jnp.int32, (BLOCK, 128), 1) == 0, 1.0, 0.0
    ).astype(BF16)
    half = BLOCK // 2
    causal = lax.broadcasted_iota(jnp.int32, (half, half), 0) >= lax.broadcasted_iota(
        jnp.int32, (half, half), 1
    )
    place = lax.broadcasted_iota(jnp.int32, (BLOCK, CODES), 0).astype(F32)
    block_scores = [
        lax.dot_general(
            queries[b * BLOCK : (b + 1) * BLOCK, lanes_of(h)],
            book,
            (((1,), (1,)), ((), ())),
            preferred_element_type=F32,
        )
        for b in range(2)
    ]
    weights, picks, tables = [], [], []
    for b in range(2):
        if b == 1:
            more, added = unpacked(early_sums, h)
            sums, counts = sums + more, counts + jnp.concatenate(added, axis=1)
        sums, counts = alive[b] * sums, alive[b] * counts
        present = counts > 0
        bias = jnp.where(present, jnp.log2(jnp.maximum(counts, 1.0)), 0.0)
        opens = jnp.where(present, -1.0, firsts[h, b : b + 1, :])
        high = jnp.floor(counts * (1.0 / 256.0)) * 256.0
        low = counts - high
        columns = []
        for r in range(4):
            lanes = slice(r * 128, (r + 1) * 128)
            columns.append(
                jnp.where(
                    square_row == 0, high[:, lanes], jnp.where(square_row == 1, low[:, lanes], 0.0)
                ).T
            )
        cache = jnp.concatenate([sums, jnp.concatenate(columns, axis=0)], axis=1).astype(BF16)
        rows = slice(b * BLOCK, (b + 1) * BLOCK)
        code_row = head_row(codes_ref, h, rows, True)
        hot = jnp.where(code_iota == code_row, 1.0, 0.0).astype(BF16)
        local = jnp.concatenate([values[rows, lanes_of(h)], ones_column], axis=1)
        scores = block_scores[b] * SCORE_TO_LOG2
        top = jnp.max(jnp.where(opens <= place, scores + bias, NEGATIVE), axis=1, keepdims=True)
        weights.append(jnp.exp2(jnp.minimum(scores - top, 0.0)).astype(BF16))
        picks.append(hot)
        tables.append(jnp.concatenate([cache, local], axis=0))
    for b in range(2):
        weight, hot, table = weights[b], picks[b], tables[b]
        near = jnp.dot(weight, hot[:, :half], preferred_element_type=F32)
        far = jnp.dot(weight[half:], hot[:, half:], preferred_element_type=F32)
        local_first = jnp.where(causal, near[:half], 0.0).astype(BF16)
        local_second = [near[half:].astype(BF16), jnp.where(causal, far, 0.0).astype(BF16)]
        upper = jnp.concatenate([weight[:half], local_first], axis=1)
        lower = jnp.concatenate([weight[half:]] + local_second, axis=1)
        for i, part in enumerate((upper, lower)):
            acc = jnp.dot(part, table[: part.shape[1]], preferred_element_type=F32)
            rows = slice(b * BLOCK + i * half, b * BLOCK + (i + 1) * half)
            out_ref[rows, :] = (acc[:, :128] / (acc[:, 128:129] + acc[:, 129:130])).astype(BF16)


def layer_kernel(
    starts_ref, codes_ref, old_ref, q_hbm, k_hbm, v_hbm, cent_hbm, out_hbm, book_hbm,
    kq, values, cents, book_ref, outs, shares, firsts, kin, vin, early_sums, kout, vout,
    kc, vc, ky, s1, kz, xsrc, kx, own, vchip, vx, vz, v2, back,
    k_sem, v_sem, q_sem, cent_sem, out_sem, share_sem, send, recv,
):
    y = lax.axis_index("dp")
    me = lax.axis_index("seq")
    c = me % 2
    x = (me // 2) % 4
    z = me // 8

    def at(dz=0, dx=0, dc=0):
        return {"seq": (((z + dz) % 4) * 4 + (x + dx) % 4) * 2 + (c + dc) % 2}

    def at_y(dy):
        return {"dp": (y + dy) % 4}

    def remote(src, dst, phase, g, device):
        return pltpu.make_async_remote_copy(
            src_ref=src, dst_ref=dst, send_sem=send.at[phase, g], recv_sem=recv.at[phase, g],
            device_id=device, device_id_type=MESH,
        )

    def four(g):
        return vchip.at[g]

    def three(g):
        return vchip.at[g, pl.ds(0, 3)]

    def three_slices(g):
        return s1.at[g, pl.ds(0, 3)]

    def three_rows(g):
        return vchip.at[g, 0, pl.ds(0, 3 * PART)]

    sizes = {
        KEY_CORE: four, VAL_CORE: four, KEY_Y: three, VAL_X: three, KEY_Z: three_slices,
        VAL_Z: three, KEY_X: three_slices, VAL_BACK: three, KEY_ZB: three_rows, KEY_YB: three,
        KEY_CB: four, VAL_CB: four,
    }

    def arrived(phase, g):
        part = sizes[phase](g)
        remote(part, part, phase, g, at(dc=1)).wait_recv()

    def left(phase, g):
        part = sizes[phase](g)
        remote(part, part, phase, g, at(dc=1)).wait_send()

    def unit_loop(body):
        def step(u, carry):
            body(u)
            return carry

        lax.fori_loop(0, 4, step, 0)

    def columns_of(g):
        return pl.ds(pl.multiple_of(g * 256, 256), 256)

    def load_keys(g):
        return pltpu.make_async_copy(k_hbm.at[0, :, columns_of(g)], kq.at[:, columns_of(g)], k_sem.at[g])

    def load_values(g):
        return pltpu.make_async_copy(v_hbm.at[0, :, columns_of(g)], values.at[:, columns_of(g)], v_sem.at[g])

    def load_queries():
        return pltpu.make_async_copy(q_hbm.at[0], kq, q_sem)

    def load_centroids(h, slot):
        return pltpu.make_async_copy(cent_hbm.at[h], cents.at[slot], cent_sem.at[slot])

    def store_out(h, slot):
        return pltpu.make_async_copy(outs.at[slot], out_hbm.at[0, :, lanes_of(h)], out_sem.at[slot])

    def store_share(h, slot):
        return pltpu.make_async_copy(shares.at[slot], book_hbm.at[h], share_sem.at[slot])

    for g in range(GROUPS):
        load_keys(g).start()
        load_values(g).start()
    for h in range(2):
        load_centroids(h, h).start()

    def sum_group(g):
        load_keys(g).wait()
        load_values(g).wait()
        for i in range(PER_GROUP):
            sum_head(
                PER_GROUP * g + i, starts_ref, codes_ref, kq, values, kin, vin, early_sums, firsts
            )

    barrier = pltpu.get_barrier_semaphore()

    def greet(device):
        pl.semaphore_signal(barrier, inc=1, device_id=device, device_id_type=MESH)

    greet(at(dc=1))
    for k in (1, 2, 3):
        greet(at(dx=k))
        greet(at(dz=k))
        greet(at_y(k))
    sum_group(0)
    pl.semaphore_wait(barrier, 10)

    def share_cores(g):
        theirs = pl.ds(8 * g + 4 * (1 - c), 4)
        remote(vin.at[theirs], vc.at[g], VAL_CORE, g, at(dc=1)).start()
        remote(kin.at[theirs], kc.at[g], KEY_CORE, g, at(dc=1)).start()

    def join(g):
        mine = 8 * g + 4 * c
        arrived(VAL_CORE, g)

        def link(u):
            ours = vin[mine + u]
            theirs = vc[g, u]
            early = jnp.where(c == 0, ours, theirs)
            late = jnp.where(c == 0, theirs, ours)
            vchip[g, u] = late + (1.0 - late[129:130, :]) * early

        unit_loop(link)
        for k in (1, 2, 3):
            remote(vchip.at[g, (x + k) % 4], vx.at[g, x], VAL_X, g, at(dx=k)).start()
        vx[g, x] = vchip[g, x]
        arrived(KEY_CORE, g)

        def add(u):
            kc[g, u] = kc[g, u] + kin[mine + u]

        unit_loop(add)
        for k in (1, 2, 3):
            remote(kc.at[g, (y + k) % 4], ky.at[g, 3 - k], KEY_Y, g, at_y(k)).start()

    def keys_y(g):
        arrived(KEY_Y, g)

        def add(i):
            rows = pl.ds(pl.multiple_of(i * PART, PART), PART)
            s1[g, i, 0:PART, :] = (kc[g, y, rows, :] + ky[g, 0, rows, :]) + (
                ky[g, 1, rows, :] + ky[g, 2, rows, :]
            )
            s1[g, i, PART:SLICE, :] = (kc[g, y, 128:136, :] + ky[g, 0, 128:136, :]) + (
                ky[g, 1, 128:136, :] + ky[g, 2, 128:136, :]
            )

        unit_loop(add)
        for k in (1, 2, 3):
            remote(s1.at[g, (z + k) % 4], kz.at[g, 3 - k], KEY_Z, g, at(dz=k)).start()

    def keys_z(g):
        arrived(KEY_Z, g)
        part = (s1[g, z] + kz[g, 0]) + (kz[g, 1] + kz[g, 2])
        xsrc[g] = part
        kx[g, x] = part
        for k in (1, 2, 3):
            remote(xsrc.at[g], kx.at[g, x], KEY_X, g, at(dx=k)).start()

    def slice_of_unit():
        return pl.ds(pl.multiple_of(z * PART, PART), PART)

    def keys_x(g):
        arrived(KEY_X, g)
        total = (kx[g, 0] + kx[g, 1]) + (kx[g, 2] + kx[g, 3])
        unit = 8 * g + 4 * c + y
        own[g] = total[0:PART]
        kout[unit, slice_of_unit(), :] = total[0:PART]
        kout[unit, 128:136, :] = total[PART:SLICE]
        for k in (1, 2, 3):
            remote(own.at[g], kout.at[unit, slice_of_unit()], KEY_ZB, g, at(dz=k)).start()

    def keys_back_z(g):
        arrived(KEY_ZB, g)
        unit = kout.at[8 * g + 4 * c + y]
        for k in (1, 2, 3):
            remote(unit, unit, KEY_YB, g, at_y(k)).start()

    def keys_back_y(g):
        arrived(KEY_YB, g)
        mine = kout.at[pl.ds(8 * g + 4 * c, 4)]
        remote(mine, mine, KEY_CB, g, at(dc=1)).start()

    def scan_row(g):
        arrived(VAL_X, g)

        def step(j, run):
            part = vx[g, j]
            vx[g, j] = run
            return part + (1.0 - part[129:130, :]) * run

        vz[g, z] = lax.fori_loop(0, 4, step, jnp.zeros((UNIT, 128), F32))
        for k in (1, 2, 3):
            remote(vz.at[g, z], vz.at[g, z], VAL_Z, g, at(dz=k)).start()

    def scan_rows(g):
        arrived(VAL_Z, g)

        def step(j, run):
            part = vz[g, j]
            return jnp.where(j < z, part + (1.0 - part[129:130, :]) * run, run)

        ahead = lax.fori_loop(0, 3, step, jnp.zeros((UNIT, 128), F32))

        def enter(j):
            part = vx[g, j]
            vx[g, j] = part + (1.0 - part[129:130, :]) * ahead

        unit_loop(enter)
        for k in (1, 2, 3):
            remote(vx.at[g, (x + k) % 4], v2.at[g, x], VAL_BACK, g, at(dx=k)).start()
        v2[g, x] = vx[g, x]

    def split(g):
        arrived(VAL_BACK, g)
        mine = 8 * g + 4 * c

        def part(u):
            early = jnp.where(c == 0, vin[mine + u], vc[g, u])
            first = v2[g, u]
            second = early + (1.0 - early[129:130, :]) * first
            vout[mine + u] = jnp.where(c == 0, first, second)
            back[g, u] = jnp.where(c == 0, second, first)

        unit_loop(part)
        remote(back.at[g], vout.at[pl.ds(mine, 4)], VAL_CB, g, at(dc=1)).start()

    def step(tick, carry):
        @pl.when((tick > 0) & (tick < GROUPS))
        def _():
            g = tick
            sum_group(g)
            share_cores(g)

            @pl.when(g == GROUPS - 1)
            def _():
                load_queries().start()

        @pl.when(tick >= ATTEND)
        def _():
            g = tick - ATTEND

            @pl.when(g == 0)
            def _():
                load_queries().wait()

            @pl.when(g > 0)
            def _():
                for i in range(PER_GROUP):
                    store_out(PER_GROUP * (g - 1) + i, i).wait()
                    store_share(PER_GROUP * (g - 1) + i, i).wait()

            for i in range(PER_GROUP):
                load_centroids(PER_GROUP * g + i, i).wait()
            arrived(KEY_CB, g)
            arrived(VAL_CB, g)
            for i in range(PER_GROUP):
                attend_head(
                    PER_GROUP * g + i, y, starts_ref, codes_ref, old_ref, kq, values, kout, vout,
                    early_sums, firsts, cents.at[i], book_ref.at[i], outs.at[i], shares.at[i],
                )
            for i in range(PER_GROUP):
                store_out(PER_GROUP * g + i, i).start()
                store_share(PER_GROUP * g + i, i).start()

            @pl.when(g + 1 < GROUPS)
            def _():
                for i in range(PER_GROUP):
                    load_centroids(PER_GROUP * (g + 1) + i, i).start()

        for when, stage in (
            (AT_YB, keys_back_y), (AT_SPLIT, split), (AT_ZB, keys_back_z), (AT_X, keys_x),
            (AT_Z, keys_z), (AT_ROWS, scan_rows), (AT_Y, keys_y), (AT_SCAN, scan_row),
            (AT_JOIN, join),
        ):

            def one(g, carry, stage=stage):
                stage(g)
                return carry

            lax.fori_loop(groups_before(when, tick), groups_before(when, tick + 1), one, 0)

        return carry

    share_cores(0)
    lax.fori_loop(1, ATTEND + GROUPS, step, 0)

    for i in range(PER_GROUP):
        store_out(HEADS - PER_GROUP + i, i).wait()
        store_share(HEADS - PER_GROUP + i, i).wait()

    def finish(g, carry):
        for phase in range(PHASES):
            left(phase, g)
        return carry

    lax.fori_loop(0, GROUPS, finish, 0)


def layer(queries, keys, values, codes, starts, centroids, old):
    anywhere = pl.BlockSpec(memory_space=pl.ANY)
    whole = pl.BlockSpec(memory_space=pltpu.VMEM)

    def units(*shape):
        return pltpu.VMEM((*shape, 128), F32)

    return pl.pallas_call(
        layer_kernel,
        name="layer",
        out_shape=(
            jax.ShapeDtypeStruct((1, TOK_DEV, HEADS * HEAD_DIM), BF16),
            jax.ShapeDtypeStruct((HEADS, CODES // 4, HEAD_DIM), F32),
        ),
        in_specs=[pl.BlockSpec(memory_space=pltpu.SMEM), whole, whole] + [anywhere] * 4,
        out_specs=[anywhere, anywhere],
        scratch_shapes=[
            pltpu.VMEM((TOK_DEV, HEADS * HEAD_DIM), BF16),
            pltpu.VMEM((TOK_DEV, HEADS * HEAD_DIM), BF16),
            units(2, CODES),
            units(2, CODES),
            pltpu.VMEM((2, TOK_DEV, HEAD_DIM), BF16),
            units(2, CODES // 4),
            pltpu.VMEM((HEADS, 8, CODES), F32),
            units(UNITS, UNIT),
            units(UNITS, UNIT),
            units(UNITS, UNIT),
            units(UNITS, UNIT),
            units(UNITS, UNIT),
            units(GROUPS, 4, UNIT),
            units(GROUPS, 4, UNIT),
            units(GROUPS, 3, UNIT),
            units(GROUPS, 4, SLICE),
            units(GROUPS, 3, SLICE),
            units(GROUPS, SLICE),
            units(GROUPS, 4, SLICE),
            units(GROUPS, PART),
            units(GROUPS, 4, UNIT),
            units(GROUPS, 4, UNIT),
            units(GROUPS, 4, UNIT),
            units(GROUPS, 4, UNIT),
            units(GROUPS, 4, UNIT),
            pltpu.SemaphoreType.DMA((GROUPS,)),
            pltpu.SemaphoreType.DMA((GROUPS,)),
            pltpu.SemaphoreType.DMA,
            pltpu.SemaphoreType.DMA((2,)),
            pltpu.SemaphoreType.DMA((2,)),
            pltpu.SemaphoreType.DMA((2,)),
            pltpu.SemaphoreType.DMA((PHASES, GROUPS)),
            pltpu.SemaphoreType.DMA((PHASES, GROUPS)),
        ],
        compiler_params=pltpu.CompilerParams(
            collective_id=0, has_side_effects=True, vmem_limit_bytes=63 << 20
        ),
    )(starts, codes, old, queries, keys, values, centroids)


def deliver_kernel(out_hbm, book_hbm, out_to, book_to, rows_held, book_held, sems):
    pieces = []
    for i in range(8):
        rows = pl.ds(i * 128, 128)
        pieces.append((out_hbm.at[0, rows], rows_held.at[rows], out_to.at[0, rows]))
    pieces.append((book_hbm, book_held, book_to))
    inward = [pltpu.make_async_copy(a, b, sems.at[0, i]) for i, (a, b, c) in enumerate(pieces)]
    outward = [pltpu.make_async_copy(b, c, sems.at[1, i]) for i, (a, b, c) in enumerate(pieces)]
    for copy in inward:
        copy.start()
    for arriving, leaving in zip(inward, outward):
        arriving.wait()
        leaving.start()
    for copy in outward:
        copy.wait()


def deliver(out, book):
    hbm = pl.BlockSpec(memory_space=pltpu.HBM)
    return pl.pallas_call(
        deliver_kernel,
        name="deliver",
        out_shape=(
            jax.ShapeDtypeStruct(out.shape, out.dtype),
            jax.ShapeDtypeStruct(book.shape, book.dtype),
        ),
        in_specs=[hbm, hbm],
        out_specs=[hbm, hbm],
        scratch_shapes=[
            pltpu.VMEM(out.shape[1:], out.dtype),
            pltpu.VMEM(book.shape, book.dtype),
            pltpu.SemaphoreType.DMA((2, 9)),
        ],
        compiler_params=pltpu.CompilerParams(vmem_limit_bytes=60 << 20),
    )(out, book)


def shards(queries, keys, values, codes, starts, old_centroids, old_counts):
    return deliver(*layer(queries, keys, values, codes, starts, old_centroids, old_counts))


def solution(mesh):
    placed = (
        P("dp", "seq", None),
        P("dp", "seq", None),
        P("dp", "seq", None),
        P("dp", None, "seq"),
        P("dp", "seq"),
        P(),
        P(),
    )
    return jax.shard_map(
        shards,
        mesh=mesh,
        in_specs=placed,
        out_specs=(P("dp", "seq", None), P(None, "dp", None)),
        check_vma=False,
    )
```
